32 devices in a mesh: sta: 8 (over z, y), seg: 4 (over x, core).
Axes of the slice: x: 2, y: 2, z: 4, core: 2. Of those that a mesh axis runs over, the one named last changes fastest.
Arguments:
- spectra: bfloat16 [48, 16, 2, 1024], P('sta', 'seg'), may hold values from -6 to 6
- observed: float32 [40, 6, 6, 512], P('sta'), may hold values from -8 to 8
- pair_table: int32 [40, 2], P('sta'), may hold values from -1 to 7, as said below
Outputs:
- gradient: float32 [48, 2, 1024], P('sta', None, 'seg')
The draws below stay inside these ranges and needn't reach their ends.
Inputs may be any that keep to these rules, and one draw needn't show every extreme that they name: `pair_table`: rows are slots; each unordered pair of station blocks p <= q of the 8 blocks stands in exactly one row as (p, q); every other row is (-1, -1).
All inputs are finite; a program needn't handle non-finite values.
Results may differ from the reference program's by a relative error of at most 0.0013.
Values may be sent and summed in bfloat16 or wider, within the bound.
No kernel may reach another device: no remote copies, remote signals or barrier semaphores. Data moves between devices by JAX's collectives and lax.ppermute only.
A program may use at most 64 MiB of HBM per device.

```python
import math
import jax
import jax.numpy as jnp
import numpy as np
from jax import lax

STA_DEV = 6
SEG_DEV = 4
F = 1024
LAGS = 512
STATIONS = 48
SEGS = 16
BLOCKS = 8
SLOTS = 40


def draw_pair_table(key, part):
    upper_first, upper_second = np.triu_indices(BLOCKS)
    block_pairs = jnp.stack([jnp.asarray(upper_first, jnp.int32), jnp.asarray(upper_second, jnp.int32)], axis=1)
    filler = -jnp.ones((SLOTS - block_pairs.shape[0], 2), jnp.int32)
    slot_rows = jnp.concatenate([block_pairs, filler], axis=0)
    shuffle_order = jax.random.permutation(jax.random.fold_in(key, 11), SLOTS)
    return slot_rows[shuffle_order]


def level_of(key, dims, cuts, smallest, top_value):
    loudness = 1.0
    for axis_at, blocks in cuts:
        steps = jax.random.uniform(jax.random.fold_in(jax.random.fold_in(key, 6), axis_at), (blocks,), jnp.float32, smallest / len(cuts), top_value / len(cuts))
        loudness = loudness * jnp.repeat(jnp.exp(steps), dims[axis_at] // blocks).reshape((-1,) + (1,) * (len(dims) - 1 - axis_at))
    return loudness


def bell_draw(rng, shape, spread, limit, shards=(), kind=jnp.bfloat16):
    factor_of = level_of(rng, shape, shards, -0.22, 0.18) if shards else 1.0
    array = jax.random.normal(rng, shape, jnp.float32) * spread * factor_of
    return jnp.minimum(jnp.maximum(array, -limit), limit).astype(kind)


def setup_inputs(seed: int = 0) -> dict:
    seeds = jax.random.split(jax.random.key(seed), 4)
    spectra = bell_draw(seeds[0], (STATIONS, SEGS, 2, F), 1.0, 6.0, ((0, 8), (1, 4)))
    observed = bell_draw(seeds[1], (SLOTS, STA_DEV, STA_DEV, LAGS), 1.5, 8.0, ((0, 8),), jnp.float32)
    pair_table = draw_pair_table(jax.random.fold_in(seeds[3], 71), 0)
    return dict(spectra=spectra, observed=observed, pair_table=pair_table)


def lag_kernel(start, count):
    frequency = (start + jnp.arange(count, dtype=jnp.int32))[:, None]
    offset = jnp.arange(LAGS, dtype=jnp.int32)[None, :] - LAGS // 2
    phase = jnp.mod(frequency * offset, 2 * F)
    angle = math.pi / F * phase.astype(jnp.float32)
    return jnp.stack([jnp.cos(angle), -jnp.sin(angle)], axis=0).astype(jnp.bfloat16)

def group_cross(left, right, groups):
    station_count = left.shape[0]
    left = left.reshape(station_count, groups, -1, 2, left.shape[-1]).astype(jnp.float32)
    right = right.reshape(station_count, groups, -1, 2, right.shape[-1]).astype(jnp.float32)
    left_real = left[:, :, :, 0][:, None]
    left_imag = left[:, :, :, 1][:, None]
    right_real = right[:, :, :, 0][None]
    right_imag = right[:, :, :, 1][None]
    cross_real = lax.optimization_barrier(jnp.sum(left_real * right_real + left_imag * right_imag, axis=3))
    cross_imag = lax.optimization_barrier(jnp.sum(left_imag * right_real - left_real * right_imag, axis=3))
    return jnp.stack([cross_real, cross_imag], axis=3).astype(jnp.bfloat16)

def pair_mask(first, second, station_count):
    row_index = jnp.arange(station_count)[:, None]
    col_index = jnp.arange(station_count)[None, :]
    keep = (first >= 0)[..., None, None] & ((first != second)[..., None, None] | (row_index < col_index))
    return keep.astype(jnp.float32)

def adjoint_terms(gamma, stacked):
    gamma_real = gamma[..., 0, :]
    gamma_imag = gamma[..., 1, :]
    stack_real = stacked[..., 0, :]
    stack_imag = stacked[..., 1, :]
    common = gamma_real * stack_real + gamma_imag * stack_imag
    twist = gamma_imag * stack_real - gamma_real * stack_imag
    left_term = jnp.stack([common.sum(-2), twist.sum(-2)], axis=-2)
    right_term = jnp.stack([common.sum(-3), -twist.sum(-3)], axis=-2)
    return (left_term, right_term)

def reference(spectra, observed, pair_table):
    kernel = lag_kernel(jnp.int32(0), F)
    exact = lax.optimization_barrier(kernel).astype(jnp.float32).reshape(2 * F, LAGS)
    scale = 1.0 / math.sqrt(F * SEGS)
    groups = SEGS // SEG_DEV

    def visit(buffer, slot):
        first, second, observe = slot
        start_left = (jnp.maximum(first, 0) * STA_DEV).astype(jnp.int32)
        start_right = (jnp.maximum(second, 0) * STA_DEV).astype(jnp.int32)
        left = lax.dynamic_slice_in_dim(spectra, start_left, STA_DEV, 0)
        right = lax.dynamic_slice_in_dim(spectra, start_right, STA_DEV, 0)
        crossed = group_cross(left, right, groups)
        stacked = lax.optimization_barrier(jnp.sum(lax.optimization_barrier(crossed).astype(jnp.float32), axis=2))
        lags = scale * jnp.dot(stacked.reshape(-1, 2 * F), exact, precision=lax.Precision.HIGHEST)
        keep = pair_mask(first, second, STA_DEV).reshape(-1, 1)
        residual = (keep * jnp.tanh(lags - observe.reshape(-1, LAGS))).astype(jnp.bfloat16)
        gamma = scale * jnp.dot(residual.astype(jnp.float32), exact.T, precision=lax.Precision.HIGHEST)
        gamma = gamma.reshape(STA_DEV, STA_DEV, 2, F)
        left_term, right_term = adjoint_terms(gamma, stacked)
        current = lax.dynamic_slice_in_dim(buffer, start_left, STA_DEV, 0)
        buffer = lax.dynamic_update_slice_in_dim(buffer, current + left_term, start_left, 0)
        current = lax.dynamic_slice_in_dim(buffer, start_right, STA_DEV, 0)
        buffer = lax.dynamic_update_slice_in_dim(buffer, current + right_term, start_right, 0)
        return (buffer, None)
    buffer = jnp.zeros((STATIONS, 2, F), jnp.float32)
    result, _ = lax.scan(visit, buffer, (pair_table[:, 0], pair_table[:, 1], observed))
    return result
```

```python
import math

import jax
import jax.numpy as jnp
from jax import lax
from jax.experimental import pallas as pl
from jax.experimental.pallas import tpu as pltpu
from jax.sharding import PartitionSpec as P

ROWS = 8

F32 = jnp.float32
BF16 = jnp.bfloat16


def call(body, outs, operands, name, scratch=(), scalars=()):
    smem = pl.BlockSpec(memory_space=pltpu.SMEM)
    vmem = pl.BlockSpec(memory_space=pltpu.VMEM)
    single = isinstance(outs, tuple)
    out_list = [outs] if single else outs
    result = pl.pallas_call(
        body,
        out_shape=[jax.ShapeDtypeStruct(s, d) for s, d in out_list],
        in_specs=[smem] * len(scalars) + [vmem] * len(operands),
        out_specs=[vmem] * len(out_list),
        scratch_shapes=list(scratch),
        name=name,
    )(*scalars, *operands)
    return result[0] if single else result


def reverse_bits(value, bits):
    out = 0
    for b in range(bits):
        out |= ((value >> b) & 1) << (bits - 1 - b)
    return out


def shift(x, axis, size, step):
    return lax.ppermute(x, axis, [(i, (i + step) % size) for i in range(size)])


def swap(x, axis, size, bit):
    return lax.ppermute(x, axis, [(i, i ^ bit) for i in range(size)])


def prepare(spectra, seg, seg_devices):
    stations, segs, parts, freqs = spectra.shape
    bits = seg_devices.bit_length() - 1
    width = freqs // seg_devices
    order = [reverse_bits(k, bits) for k in range(seg_devices)]
    aligned = width % 128 == 0
    if not aligned:
        chunks = spectra.reshape(stations, segs, parts, seg_devices, width)
        spectra = jnp.take(chunks, jnp.array(order) ^ seg[0], axis=3).reshape(spectra.shape)

    def body(seg_ref, x_ref, o_ref, tmp):
        for n in range(stations):
            for t in range(segs):
                value = x_ref[n, t].astype(F32)
                for c in range(parts):
                    tmp[pl.ds((t * parts + c) * stations + n, 1), :] = value[c : c + 1]
        for k in range(seg_devices):
            to = pl.ds(k * width, width)
            if aligned:
                at = pl.ds(pl.multiple_of((seg_ref[0] ^ order[k]) * width, 128), width)
            else:
                at = to
            o_ref[:, to] = tmp[:, at].astype(BF16)

    rows = segs * parts * stations
    return call(body, ((rows, freqs), BF16), [spectra], "prepare", [pltpu.VMEM((rows, freqs), F32)], [seg])


def lag_kernel(freqs, lags, seg, seg_devices):
    bits = seg_devices.bit_length() - 1
    width = freqs // seg_devices
    order = [reverse_bits(k, bits) for k in range(seg_devices)]
    fine = math.gcd(width, 64)
    coarse = freqs // fine
    period = 2 * freqs

    def body(seg_ref, o_ref, cos_ref, sin_ref):
        def table(count, step):
            f = lax.broadcasted_iota(jnp.int32, (count, lags), 0) * step
            offset = lax.broadcasted_iota(jnp.int32, (count, lags), 1) - lags // 2
            phase = (f * offset) & (period - 1)
            angle = math.pi / freqs * phase.astype(F32)
            return jnp.cos(angle), jnp.sin(angle)

        fine_cos, fine_sin = table(fine, 1)
        big_cos, big_sin = table(coarse, fine)
        cos_ref[...] = big_cos
        sin_ref[...] = big_sin
        for k in range(seg_devices):
            for s in range(width // fine):
                row = (seg_ref[0] ^ order[k]) * (width // fine) + s
                c = cos_ref[pl.ds(row, 1), :]
                d = sin_ref[pl.ds(row, 1), :]
                at = k * width + s * fine
                o_ref[pl.ds(at, fine), :] = (fine_cos * c - fine_sin * d).astype(BF16)
                o_ref[pl.ds(freqs + at, fine), :] = (-(fine_sin * c + fine_cos * d)).astype(BF16)

    return call(
        body,
        ((2 * freqs, lags), BF16),
        [],
        "lag_kernel",
        [pltpu.VMEM((coarse, lags), F32)] * 2,
        [seg],
    )


def forward(blocks, kernel, table, place, segs, stations, slots):
    count = len(blocks)
    freqs = blocks[0].shape[1]
    lags = kernel.shape[1]
    half = lags // 2
    rows = slots * stations * ROWS
    lane = 256

    def body(table_ref, place_ref, *refs):
        block_refs = refs[:count]
        k_ref, cross_ref, mine_ref, send_ref, x_ref, lag_ref = refs[count:]
        own = place_ref[0]
        pad = jnp.zeros((ROWS - stations, freqs), F32)
        for d in range(count):
            at = lax.rem(own + (count - d), count)
            value = block_refs[d][...].astype(F32)
            for r in range(2 * segs):
                x_ref[at, r] = jnp.concatenate([value[r * stations : (r + 1) * stations], pad], axis=0)

        def one_slot(r, carry):
            p = jnp.maximum(table_ref[r, 0], 0)
            q = jnp.maximum(table_ref[r, 1], 0)
            for f in range(0, freqs, lane):
                fs = pl.ds(f, lane)
                right = [x_ref[q, k, :, fs] for k in range(2 * segs)]
                real, imag = [], []
                for a in range(stations):
                    re = im = None
                    for t in range(segs):
                        x0 = x_ref[p, 2 * t, pl.ds(a, 1), fs]
                        x1 = x_ref[p, 2 * t + 1, pl.ds(a, 1), fs]
                        y0, y1 = right[2 * t], right[2 * t + 1]
                        u = x0 * y0 + x1 * y1
                        v = x1 * y0 - x0 * y1
                        re = u if re is None else re + u
                        im = v if im is None else im + v
                    real.append(re)
                    imag.append(im)
                for a in range(0, stations, 2):
                    at = pl.multiple_of((r * stations + a) * ROWS, 2 * ROWS)
                    cross_ref[pl.ds(at, 2 * ROWS), fs] = jnp.concatenate(real[a : a + 2], axis=0).astype(BF16)
                    cross_ref[pl.ds(at, 2 * ROWS), pl.ds(freqs + f, lane)] = jnp.concatenate(
                        imag[a : a + 2], axis=0
                    ).astype(BF16)
            return carry

        lax.fori_loop(0, slots, one_slot, 0)
        lag_ref[...] = jnp.dot(cross_ref[...], k_ref[...], preferred_element_type=F32)
        here = pl.ds(pl.multiple_of(place_ref[1] * half, 128), half)
        there = pl.ds(pl.multiple_of((1 - place_ref[1]) * half, 128), half)
        for k in range(slots * stations):
            mine_ref[pl.ds(k * stations, stations), :] = lag_ref[pl.ds(k * ROWS, stations), here]
            send_ref[pl.ds(k * stations, stations), :] = lag_ref[pl.ds(k * ROWS, stations), there]

    small = (slots * stations * stations, half)
    return call(
        body,
        [((rows, 2 * freqs), BF16), (small, F32), (small, F32)],
        [*blocks, kernel],
        "forward",
        [pltpu.VMEM((count, 2 * segs, ROWS, freqs), F32), pltpu.VMEM((rows, lags), F32)],
        [table, place],
    )


def add(a, b, name):
    def body(a_ref, b_ref, o_ref):
        o_ref[...] = a_ref[...] + b_ref[...]

    return call(body, (a.shape, a.dtype), [a, b], name)


def misfit(a, b, observed, table, place, scale):
    slots, stations, _, lags = observed.shape
    half = lags // 2

    def body(table_ref, place_ref, a_ref, b_ref, obs_ref, o_ref):
        here = pl.ds(pl.multiple_of(place_ref[1] * half, 128), half)
        column = lax.broadcasted_iota(jnp.int32, (stations, half), 0)
        pad = jnp.zeros((ROWS - stations, half), F32)
        for r in range(slots):
            p, q = table_ref[r, 0], table_ref[r, 1]
            low = jnp.where(p < 0, stations, jnp.where(p != q, -1, 0))
            same = jnp.where(p == q, 1, 0)
            tiles = []
            for row in range(stations):
                at = pl.ds((r * stations + row) * stations, stations)
                value = jnp.tanh(scale * (a_ref[at, :] + b_ref[at, :]) - obs_ref[r, row, :, here])
                value = jnp.where(column > low + same * row, value, 0.0)
                tiles += [value, pad]
            for row in range(0, stations, 2):
                at = pl.ds((r * stations + row) * ROWS, 2 * ROWS)
                o_ref[at, :] = jnp.concatenate(tiles[2 * row : 2 * row + 4], axis=0).astype(BF16)

    return call(body, ((slots * stations * ROWS, half), BF16), [a, b, observed], "misfit", (), [table, place])


def backward(mine, other, cross, kernel, table, place, slots, stations, blocks, scale):
    rows, half = mine.shape
    freqs = kernel.shape[0] // 2
    lane = 256
    outer = blocks // 2
    targets = blocks * stations
    part = outer * stations

    def body(table_ref, place_ref, mine_ref, other_ref, cross_ref, k_ref, keep_ref, send_ref):
        own = place_ref[0]
        m = lax.broadcasted_iota(jnp.int32, (targets, rows), 0)
        n = m % stations
        group = m // stations
        block = 2 * ((own // 2 + group % outer) % outer) + ((own % 2) ^ (group // outer))
        k = lax.broadcasted_iota(jnp.int32, (targets, rows), 1)
        b = k % ROWS
        a = (k // ROWS) % stations
        r = k // (ROWS * stations)
        first = jnp.full((targets, rows), -1, jnp.int32)
        second = jnp.full((targets, rows), -1, jnp.int32)
        for s in range(slots):
            first = jnp.where(r == s, table_ref[s, 0], first)
            second = jnp.where(r == s, table_ref[s, 1], second)
        left = jnp.where((first == block) & (a == n), 1.0, 0.0)
        right = jnp.where((second == block) & (b == n), 1.0, 0.0)
        plus = (left + right).astype(BF16)
        minus = (left - right).astype(BF16)
        here = pl.ds(pl.multiple_of(place_ref[1] * half, 128), half)
        there = pl.ds(pl.multiple_of((1 - place_ref[1]) * half, 128), half)
        res_mine = mine_ref[...]
        res_other = other_ref[...]
        contract = (((1,), (1,)), ((), ()))

        def gamma(at):
            one = lax.dot_general(res_mine, k_ref[at, here], contract, preferred_element_type=F32)
            two = lax.dot_general(res_other, k_ref[at, there], contract, preferred_element_type=F32)
            return scale * (one + two)

        def total(select, value):
            high = value.astype(BF16)
            rest = value - high.astype(F32)
            middle = rest.astype(BF16)
            low = (rest - middle.astype(F32)).astype(BF16)
            out = jnp.dot(select, high, preferred_element_type=F32)
            out = out + jnp.dot(select, middle, preferred_element_type=F32)
            return out + jnp.dot(select, low, preferred_element_type=F32)

        for f in range(0, freqs, lane):
            real = gamma(pl.ds(f, lane))
            imag = gamma(pl.ds(freqs + f, lane))
            stack_real = cross_ref[:, pl.ds(f, lane)].astype(F32)
            stack_imag = cross_ref[:, pl.ds(freqs + f, lane)].astype(F32)
            common = total(plus, real * stack_real + imag * stack_imag)
            twist = total(minus, imag * stack_real - real * stack_imag)
            into = keep_ref if f < freqs // 2 else send_ref
            at = pl.ds(f % (freqs // 2), lane)
            for y in range(2):
                into[pl.ds((2 * y) * part, part), at] = common[y * part : (y + 1) * part]
                into[pl.ds((2 * y + 1) * part, part), at] = twist[y * part : (y + 1) * part]

    shape = ((2 * targets, freqs // 2), F32)
    return call(body, [shape, shape], [mine, other, cross, kernel], "backward", (), [table, place])


def add_split_lanes(a, b):
    rows, width = a.shape
    half = width // 2

    def body(a_ref, b_ref, keep_ref, send_ref):
        for ref, at in ((keep_ref, 0), (send_ref, half)):
            ref[...] = a_ref[:, pl.ds(at, half)] + b_ref[:, pl.ds(at, half)]

    return call(body, [((rows, half), F32)] * 2, [a, b], "add_split_lanes")


def add_split_rows(a, b):
    rows, width = a.shape
    half = rows // 2

    def body(a_ref, b_ref, keep_ref, send_ref):
        for ref, at in ((keep_ref, 0), (send_ref, half)):
            ref[...] = a_ref[pl.ds(at, half), :] + b_ref[pl.ds(at, half), :]

    return call(body, [((half, width), F32)] * 2, [a, b], "add_split_rows")


def add_split_blocks(a, b, stations):
    rows, width = a.shape
    count = rows // (2 * stations)

    def body(a_ref, b_ref, *out_refs):
        for d in range(count):
            for c in range(2):
                at = pl.ds((c * count + d) * stations, stations)
                out_refs[d][c] = a_ref[at, :] + b_ref[at, :]

    return call(body, [((2, stations, width), F32)] * count, [a, b], "add_split_blocks")


def finish(pieces):
    _, stations, width = pieces[0].shape

    def body(*refs):
        o_ref = refs[-1]
        for c in range(2):
            value = refs[0][c]
            for ref in refs[1:-1]:
                value = value + ref[c]
            for n in range(stations):
                o_ref[n, pl.ds(c, 1), :] = value[n : n + 1]

    return call(body, ((stations, 2, width), F32), pieces, "finish")


def on_device(spectra, observed, pair_table):
    stations, segs, _, freqs = spectra.shape
    slots = pair_table.shape[0]
    lags = observed.shape[3]
    sta_devices = lax.axis_size("sta")
    seg_devices = lax.axis_size("seg")
    bits = seg_devices.bit_length() - 1
    scale = 1.0 / math.sqrt(freqs * segs * seg_devices)
    seg = lax.axis_index("seg").astype(jnp.int32)
    sta = lax.axis_index("sta").astype(jnp.int32)
    seg_at = jnp.stack([seg])
    place = jnp.stack([sta, seg % 2])

    block = prepare(spectra, seg_at, seg_devices)
    blocks = [block] + [shift(block, "sta", sta_devices, d) for d in range(1, sta_devices)]
    kernel = lag_kernel(freqs, lags, seg_at, seg_devices)
    cross, mine, send = forward(blocks, kernel, pair_table, place, segs, stations, slots)
    total = add(mine, swap(send, "seg", seg_devices, 1), "add_core")
    for b in range(1, bits - 1):
        total = add(total, swap(total, "seg", seg_devices, 1 << b), "add_lags")
    last = swap(total, "seg", seg_devices, 1 << (bits - 1))
    residual = misfit(total, last, observed, pair_table, place, scale)
    other = swap(residual, "seg", seg_devices, 1)
    keep, send = backward(
        residual, other, cross, kernel, pair_table, place, slots, stations, sta_devices, scale
    )
    for b in range(bits - 1):
        keep, send = add_split_lanes(keep, swap(send, "seg", seg_devices, 1 << b))
    keep, send = add_split_rows(keep, swap(send, "seg", seg_devices, 1 << (bits - 1)))
    pieces = add_split_blocks(keep, swap(send, "sta", sta_devices, 1), stations)
    arrived = [shift(piece, "sta", sta_devices, 2 * d) for d, piece in enumerate(pieces) if d]
    return finish([pieces[0], *arrived])


def solution(mesh):
    placed = (P("sta", "seg", None, None), P("sta", None, None, None), P("sta", None))
    return jax.shard_map(
        on_device, mesh=mesh, in_specs=placed, out_specs=P("sta", None, "seg"), check_vma=False
    )
```

```python
import math

import jax
import jax.numpy as jnp
from jax import lax
from jax.experimental import pallas as pl
from jax.experimental.pallas import tpu as pltpu
from jax.sharding import PartitionSpec as P

ROWS = 8

F32 = jnp.float32
BF16 = jnp.bfloat16


def call(body, outs, operands, name, scratch=(), scalars=(), inside=True, limit=24 << 20):
    smem = pl.BlockSpec(memory_space=pltpu.SMEM)
    vmem = pl.BlockSpec(memory_space=pltpu.VMEM)
    operands = [pltpu.with_memory_space_constraint(x, pltpu.VMEM) for x in operands]
    single = isinstance(outs, tuple)
    out_list = [outs] if single else outs
    result = pl.pallas_call(
        body,
        out_shape=[pltpu.VMEM(s, d) if inside else jax.ShapeDtypeStruct(s, d) for s, d in out_list],
        in_specs=[smem] * len(scalars) + [vmem] * len(operands),
        out_specs=[vmem] * len(out_list),
        scratch_shapes=list(scratch),
        name=name,
        compiler_params=pltpu.CompilerParams(vmem_limit_bytes=limit),
    )(*scalars, *operands)
    return result[0] if single else result


def reverse_bits(value, bits):
    out = 0
    for b in range(bits):
        out |= ((value >> b) & 1) << (bits - 1 - b)
    return out


def shift(x, axis, size, step):
    return lax.ppermute(x, axis, [(i, (i + step) % size) for i in range(size)])


def swap(x, axis, size, bit):
    return lax.ppermute(x, axis, [(i, i ^ bit) for i in range(size)])


def prepare(spectra, seg, seg_devices):
    stations, segs, parts, freqs = spectra.shape
    bits = seg_devices.bit_length() - 1
    width = freqs // seg_devices
    order = [reverse_bits(k, bits) for k in range(seg_devices)]
    aligned = width % 128 == 0
    if not aligned:
        chunks = spectra.reshape(stations, segs, parts, seg_devices, width)
        spectra = jnp.take(chunks, jnp.array(order) ^ seg[0], axis=3).reshape(spectra.shape)

    def body(seg_ref, x_ref, o_ref, tmp):
        for n in range(stations):
            for t in range(segs):
                value = x_ref[n, t].astype(F32)
                for c in range(parts):
                    tmp[pl.ds((t * parts + c) * stations + n, 1), :] = value[c : c + 1]
        for k in range(seg_devices):
            to = pl.ds(k * width, width)
            if aligned:
                at = pl.ds(pl.multiple_of((seg_ref[0] ^ order[k]) * width, 128), width)
            else:
                at = to
            o_ref[:, to] = tmp[:, at].astype(BF16)

    rows = segs * parts * stations
    return call(body, ((rows, freqs), BF16), [spectra], "prepare", [pltpu.VMEM((rows, freqs), F32)], [seg])


def lag_kernel(freqs, lags, seg, seg_devices):
    bits = seg_devices.bit_length() - 1
    width = freqs // seg_devices
    order = [reverse_bits(k, bits) for k in range(seg_devices)]
    fine = math.gcd(width, 64)
    coarse = freqs // fine
    period = 2 * freqs

    def body(seg_ref, o_ref, cos_ref, sin_ref):
        def table(count, step):
            f = lax.broadcasted_iota(jnp.int32, (count, lags), 0) * step
            offset = lax.broadcasted_iota(jnp.int32, (count, lags), 1) - lags // 2
            phase = (f * offset) & (period - 1)
            angle = math.pi / freqs * phase.astype(F32)
            return jnp.cos(angle), jnp.sin(angle)

        fine_cos, fine_sin = table(fine, 1)
        big_cos, big_sin = table(coarse, fine)
        cos_ref[...] = big_cos
        sin_ref[...] = big_sin
        for k in range(seg_devices):
            for s in range(width // fine):
                row = (seg_ref[0] ^ order[k]) * (width // fine) + s
                c = cos_ref[pl.ds(row, 1), :]
                d = sin_ref[pl.ds(row, 1), :]
                at = k * width + s * fine
                o_ref[pl.ds(at, fine), :] = (fine_cos * c - fine_sin * d).astype(BF16)
                o_ref[pl.ds(freqs + at, fine), :] = (-(fine_sin * c + fine_cos * d)).astype(BF16)

    return call(
        body,
        ((2 * freqs, lags), BF16),
        [],
        "lag_kernel",
        [pltpu.VMEM((coarse, lags), F32)] * 2,
        [seg],
    )


def forward(blocks, kernel, table, place, seg, segs, stations, slots):
    count = len(blocks)
    freqs = blocks[0].shape[1]
    lags = kernel.shape[1]
    half = lags // 2
    rows = slots * stations * ROWS
    lane = 256

    def body(table_ref, place_ref, seg_ref, *refs):
        block_refs = refs[:count]
        k_ref, cross_ref, mine_ref, send_ref, x_ref, lag_ref = refs[count:]
        own = place_ref[0]
        pad = jnp.zeros((ROWS - stations, freqs), F32)
        for d in range(count):
            at = lax.rem(own + (count - d), count)
            value = block_refs[d][...].astype(F32)
            for r in range(2 * segs):
                x_ref[at, r] = jnp.concatenate([value[r * stations : (r + 1) * stations], pad], axis=0)

        def one_slot(r, carry):
            p = jnp.maximum(table_ref[0, r], 0)
            q = jnp.maximum(table_ref[1, r], 0)
            for f in range(0, freqs, lane):
                fs = pl.ds(f, lane)
                right = [x_ref[q, k, :, fs] for k in range(2 * segs)]
                real, imag = [], []
                for a in range(stations):
                    re = im = None
                    for t in range(segs):
                        x0 = x_ref[p, 2 * t, pl.ds(a, 1), fs]
                        x1 = x_ref[p, 2 * t + 1, pl.ds(a, 1), fs]
                        y0, y1 = right[2 * t], right[2 * t + 1]
                        u = x0 * y0 + x1 * y1
                        v = x1 * y0 - x0 * y1
                        re = u if re is None else re + u
                        im = v if im is None else im + v
                    real.append(re)
                    imag.append(im)
                for a in range(0, stations, 2):
                    at = pl.multiple_of((r * stations + a) * ROWS, 2 * ROWS)
                    cross_ref[pl.ds(at, 2 * ROWS), fs] = jnp.concatenate(real[a : a + 2], axis=0).astype(BF16)
                    cross_ref[pl.ds(at, 2 * ROWS), pl.ds(freqs + f, lane)] = jnp.concatenate(
                        imag[a : a + 2], axis=0
                    ).astype(BF16)
            return carry

        lax.fori_loop(0, slots, one_slot, 0)
        lag_ref[...] = jnp.dot(cross_ref[...], k_ref[...], preferred_element_type=F32)
        here = pl.ds(pl.multiple_of((seg_ref[0] & 1) * half, 128), half)
        there = pl.ds(pl.multiple_of((1 - (seg_ref[0] & 1)) * half, 128), half)
        for k in range(slots * stations):
            mine_ref[pl.ds(k * stations, stations), :] = lag_ref[pl.ds(k * ROWS, stations), here]
            send_ref[pl.ds(k * stations, stations), :] = lag_ref[pl.ds(k * ROWS, stations), there]

    small = (slots * stations * stations, half)
    return call(
        body,
        [((rows, 2 * freqs), BF16), (small, F32), (small, F32)],
        [*blocks, kernel],
        "forward",
        [pltpu.VMEM((count, 2 * segs, ROWS, freqs), F32), pltpu.VMEM((rows, lags), F32)],
        [table, place, seg],
    )


def misfit(a, b, observed, table, place, seg, scale):
    slots, stations, _, lags = observed.shape
    half = lags // 2

    def body(table_ref, place_ref, seg_ref, a_ref, b_ref, obs_ref, o_ref):
        here = pl.ds(pl.multiple_of((seg_ref[0] & 1) * half, 128), half)
        column = lax.broadcasted_iota(jnp.int32, (stations, half), 0)
        pad = jnp.zeros((ROWS - stations, half), F32)
        for r in range(slots):
            p, q = table_ref[0, r], table_ref[1, r]
            low = jnp.where(p < 0, stations, jnp.where(p != q, -1, 0))
            same = jnp.where(p == q, 1, 0)
            tiles = []
            for row in range(stations):
                at = pl.ds((r * stations + row) * stations, stations)
                value = jnp.tanh(scale * (a_ref[at, :] + b_ref[at, :]) - obs_ref[r, row, :, here])
                value = jnp.where(column > low + same * row, value, 0.0)
                tiles += [value, pad]
            for row in range(0, stations, 2):
                at = pl.ds((r * stations + row) * ROWS, 2 * ROWS)
                o_ref[at, :] = jnp.concatenate(tiles[2 * row : 2 * row + 4], axis=0).astype(BF16)

    return call(body, ((slots * stations * ROWS, half), BF16), [a, b, observed], "misfit", (), [table, place, seg])


def backward(mine, other, cross, kernel, table, place, seg, slots, stations, blocks, scale):
    rows, half = mine.shape
    freqs = kernel.shape[0] // 2
    lane = 256
    outer = blocks // 2
    targets = blocks * stations
    part = outer * stations

    def body(table_ref, place_ref, seg_ref, mine_ref, other_ref, cross_ref, k_ref, keep_ref, send_ref):
        own = place_ref[0]
        m = lax.broadcasted_iota(jnp.int32, (targets, rows), 0)
        n = m % stations
        group = m // stations
        block = 2 * ((own // 2 + group % outer) % outer) + ((own % 2) ^ (group // outer))
        k = lax.broadcasted_iota(jnp.int32, (targets, rows), 1)
        b = k % ROWS
        a = (k // ROWS) % stations
        r = k // (ROWS * stations)
        first = jnp.full((targets, rows), -1, jnp.int32)
        second = jnp.full((targets, rows), -1, jnp.int32)
        for s in range(slots):
            first = jnp.where(r == s, table_ref[0, s], first)
            second = jnp.where(r == s, table_ref[1, s], second)
        left = jnp.where((first == block) & (a == n), 1.0, 0.0)
        right = jnp.where((second == block) & (b == n), 1.0, 0.0)
        plus = (left + right).astype(BF16)
        minus = (left - right).astype(BF16)
        here = pl.ds(pl.multiple_of((seg_ref[0] & 1) * half, 128), half)
        there = pl.ds(pl.multiple_of((1 - (seg_ref[0] & 1)) * half, 128), half)
        res_mine = mine_ref[...]
        res_other = other_ref[...]
        contract = (((1,), (1,)), ((), ()))

        def gamma(at):
            one = lax.dot_general(res_mine, k_ref[at, here], contract, preferred_element_type=F32)
            two = lax.dot_general(res_other, k_ref[at, there], contract, preferred_element_type=F32)
            return scale * (one + two)

        def total(select, value):
            high = value.astype(BF16)
            rest = value - high.astype(F32)
            middle = rest.astype(BF16)
            low = (rest - middle.astype(F32)).astype(BF16)
            out = jnp.dot(select, high, preferred_element_type=F32)
            out = out + jnp.dot(select, middle, preferred_element_type=F32)
            return out + jnp.dot(select, low, preferred_element_type=F32)

        for f in range(0, freqs, lane):
            real = gamma(pl.ds(f, lane))
            imag = gamma(pl.ds(freqs + f, lane))
            stack_real = cross_ref[:, pl.ds(f, lane)].astype(F32)
            stack_imag = cross_ref[:, pl.ds(freqs + f, lane)].astype(F32)
            common = total(plus, real * stack_real + imag * stack_imag)
            twist = total(minus, imag * stack_real - real * stack_imag)
            into = keep_ref if f < freqs // 2 else send_ref
            at = pl.ds(f % (freqs // 2), lane)
            for y in range(2):
                into[pl.ds((2 * y) * part, part), at] = common[y * part : (y + 1) * part]
                into[pl.ds((2 * y + 1) * part, part), at] = twist[y * part : (y + 1) * part]

    shape = ((2 * targets, freqs // 2), F32)
    return call(body, [shape, shape], [mine, other, cross, kernel], "backward", (), [table, place, seg])


def add_split(a, b, axis):
    half = a.shape[axis] // 2
    parts = [lax.slice_in_dim(a, k, k + half, axis=axis) + lax.slice_in_dim(b, k, k + half, axis=axis) for k in (0, half)]
    return parts


def add_split_blocks(a, b, stations):
    rows, width = a.shape
    count = rows // (2 * stations)

    def body(a_ref, b_ref, *out_refs):
        for d in range(count):
            for c in range(2):
                at = pl.ds((c * count + d) * stations, stations)
                out_refs[d][c] = a_ref[at, :] + b_ref[at, :]

    return call(body, [((2, stations, width), F32)] * count, [a, b], "add_split_blocks")


def finish(pieces):
    _, stations, width = pieces[0].shape

    def body(*refs):
        o_ref = refs[-1]
        for c in range(2):
            value = refs[0][c]
            for ref in refs[1:-1]:
                value = value + ref[c]
            for n in range(stations):
                o_ref[n, pl.ds(c, 1), :] = value[n : n + 1]

    return call(body, ((stations, 2, width), F32), pieces, "finish", inside=False)


def on_device(spectra, observed, pair_table):
    stations, segs, _, freqs = spectra.shape
    slots = pair_table.shape[0]
    lags = observed.shape[3]
    sta_devices = lax.axis_size("sta")
    seg_devices = lax.axis_size("seg")
    bits = seg_devices.bit_length() - 1
    scale = 1.0 / math.sqrt(freqs * segs * seg_devices)
    seg = lax.axis_index("seg").astype(jnp.int32)
    sta = lax.axis_index("sta").astype(jnp.int32)
    seg_at = seg.reshape(1)
    place = sta.reshape(1)
    table = pair_table.T

    block = prepare(spectra, seg_at, seg_devices)
    blocks = [block] + [shift(block, "sta", sta_devices, d) for d in range(1, sta_devices)]
    kernel = lag_kernel(freqs, lags, seg_at, seg_devices)
    cross, mine, send = forward(blocks, kernel, table, place, seg_at, segs, stations, slots)
    total = mine + swap(send, "seg", seg_devices, 1)
    for b in range(1, bits - 1):
        total = total + swap(total, "seg", seg_devices, 1 << b)
    last = swap(total, "seg", seg_devices, 1 << (bits - 1))
    residual = misfit(total, last, observed, table, place, seg_at, scale)
    other = swap(residual, "seg", seg_devices, 1)
    keep, send = backward(
        residual, other, cross, kernel, table, place, seg_at, slots, stations, sta_devices, scale
    )
    for b in range(bits - 1):
        keep, send = add_split(keep, swap(send, "seg", seg_devices, 1 << b), 1)
    keep, send = add_split(keep, swap(send, "seg", seg_devices, 1 << (bits - 1)), 0)
    pieces = add_split_blocks(keep, swap(send, "sta", sta_devices, 1), stations)
    arrived = [shift(piece, "sta", sta_devices, 2 * d) for d, piece in enumerate(pieces) if d]
    return finish([pieces[0], *arrived])


def solution(mesh):
    placed = (P("sta", "seg", None, None), P("sta", None, None, None), P("sta", None))
    return jax.shard_map(
        on_device, mesh=mesh, in_specs=placed, out_specs=P("sta", None, "seg"), check_vma=False
    )
```

```python
import math

import jax
import jax.numpy as jnp
from jax import lax
from jax.experimental import pallas as pl
from jax.experimental.pallas import tpu as pltpu
from jax.sharding import PartitionSpec as P

ROWS = 8

F32 = jnp.float32
BF16 = jnp.bfloat16


def call(body, outs, operands, name, scratch=(), scalars=(), inside=True, limit=24 << 20):
    smem = pl.BlockSpec(memory_space=pltpu.SMEM)
    vmem = pl.BlockSpec(memory_space=pltpu.VMEM)
    operands = [pltpu.with_memory_space_constraint(x, pltpu.VMEM) for x in operands]
    single = isinstance(outs, tuple)
    out_list = [outs] if single else outs
    result = pl.pallas_call(
        body,
        out_shape=[pltpu.VMEM(s, d) if inside else jax.ShapeDtypeStruct(s, d) for s, d in out_list],
        in_specs=[smem] * len(scalars) + [vmem] * len(operands),
        out_specs=[vmem] * len(out_list),
        scratch_shapes=list(scratch),
        name=name,
        compiler_params=pltpu.CompilerParams(vmem_limit_bytes=limit),
    )(*scalars, *operands)
    return result[0] if single else result


def reverse_bits(value, bits):
    out = 0
    for b in range(bits):
        out |= ((value >> b) & 1) << (bits - 1 - b)
    return out


def shift(x, axis, size, step):
    return lax.ppermute(x, axis, [(i, (i + step) % size) for i in range(size)])


def swap(x, axis, size, bit):
    return lax.ppermute(x, axis, [(i, i ^ bit) for i in range(size)])


def prepare(spectra, seg, seg_devices):
    stations, segs, parts, freqs = spectra.shape
    bits = seg_devices.bit_length() - 1
    width = freqs // seg_devices
    order = [reverse_bits(k, bits) for k in range(seg_devices)]
    aligned = width % 128 == 0
    if not aligned:
        chunks = spectra.reshape(stations, segs, parts, seg_devices, width)
        spectra = jnp.take(chunks, jnp.array(order) ^ seg[0], axis=3).reshape(spectra.shape)

    def body(seg_ref, x_ref, o_ref, tmp):
        for n in range(stations):
            for t in range(segs):
                value = x_ref[n, t].astype(F32)
                for c in range(parts):
                    tmp[pl.ds((t * parts + c) * stations + n, 1), :] = value[c : c + 1]
        for k in range(seg_devices):
            to = pl.ds(k * width, width)
            if aligned:
                at = pl.ds(pl.multiple_of((seg_ref[0] ^ order[k]) * width, 128), width)
            else:
                at = to
            o_ref[:, to] = tmp[:, at].astype(BF16)

    rows = segs * parts * stations
    return call(body, ((rows, freqs), BF16), [spectra], "prepare", [pltpu.VMEM((rows, freqs), F32)], [seg])


def lag_kernel(freqs, lags, seg, seg_devices):
    bits = seg_devices.bit_length() - 1
    width = freqs // seg_devices
    order = [reverse_bits(k, bits) for k in range(seg_devices)]
    fine = math.gcd(width, 64)
    coarse = freqs // fine
    period = 2 * freqs

    def body(seg_ref, o_ref, cos_ref, sin_ref):
        def table(count, step):
            f = lax.broadcasted_iota(jnp.int32, (count, lags), 0) * step
            offset = lax.broadcasted_iota(jnp.int32, (count, lags), 1) - lags // 2
            phase = (f * offset) & (period - 1)
            angle = math.pi / freqs * phase.astype(F32)
            return jnp.cos(angle), jnp.sin(angle)

        fine_cos, fine_sin = table(fine, 1)
        big_cos, big_sin = table(coarse, fine)
        cos_ref[...] = big_cos
        sin_ref[...] = big_sin
        for k in range(seg_devices):
            for s in range(width // fine):
                row = (seg_ref[0] ^ order[k]) * (width // fine) + s
                c = cos_ref[pl.ds(row, 1), :]
                d = sin_ref[pl.ds(row, 1), :]
                at = k * width + s * fine
                o_ref[pl.ds(at, fine), :] = (fine_cos * c - fine_sin * d).astype(BF16)
                o_ref[pl.ds(freqs + at, fine), :] = (-(fine_sin * c + fine_cos * d)).astype(BF16)

    return call(
        body,
        ((2 * freqs, lags), BF16),
        [],
        "lag_kernel",
        [pltpu.VMEM((coarse, lags), F32)] * 2,
        [seg],
    )


def forward(blocks, order, kernel, table, place, seg, segs, stations, slots):
    count = len(blocks)
    freqs = blocks[0].shape[1]
    lags = kernel.shape[1]
    half = lags // 2
    rows = slots * stations * ROWS
    lane = 256

    def body(table_ref, place_ref, seg_ref, *refs):
        block_refs = refs[:count]
        k_ref, cross_ref, mine_ref, send_ref, x_ref, lag_ref = refs[count:]
        own = place_ref[0]
        pad = jnp.zeros((ROWS - stations, freqs), F32)
        for k, d in enumerate(order):
            at = own ^ d
            value = block_refs[k][...].astype(F32)
            for r in range(2 * segs):
                x_ref[at, r] = jnp.concatenate([value[r * stations : (r + 1) * stations], pad], axis=0)

        def one_slot(r, carry):
            p = jnp.maximum(table_ref[0, r], 0)
            q = jnp.maximum(table_ref[1, r], 0)
            for f in range(0, freqs, lane):
                fs = pl.ds(f, lane)
                right = [x_ref[q, k, :, fs] for k in range(2 * segs)]
                real, imag = [], []
                for a in range(stations):
                    re = im = None
                    for t in range(segs):
                        x0 = x_ref[p, 2 * t, pl.ds(a, 1), fs]
                        x1 = x_ref[p, 2 * t + 1, pl.ds(a, 1), fs]
                        y0, y1 = right[2 * t], right[2 * t + 1]
                        u = x0 * y0 + x1 * y1
                        v = x1 * y0 - x0 * y1
                        re = u if re is None else re + u
                        im = v if im is None else im + v
                    real.append(re)
                    imag.append(im)
                for a in range(0, stations, 2):
                    at = pl.multiple_of((r * stations + a) * ROWS, 2 * ROWS)
                    cross_ref[pl.ds(at, 2 * ROWS), fs] = jnp.concatenate(real[a : a + 2], axis=0).astype(BF16)
                    cross_ref[pl.ds(at, 2 * ROWS), pl.ds(freqs + f, lane)] = jnp.concatenate(
                        imag[a : a + 2], axis=0
                    ).astype(BF16)
            return carry

        lax.fori_loop(0, slots, one_slot, 0)
        lag_ref[...] = jnp.dot(cross_ref[...], k_ref[...], preferred_element_type=F32)
        here = pl.ds(pl.multiple_of((seg_ref[0] & 1) * half, 128), half)
        there = pl.ds(pl.multiple_of((1 - (seg_ref[0] & 1)) * half, 128), half)
        for k in range(slots * stations):
            mine_ref[pl.ds(k * stations, stations), :] = lag_ref[pl.ds(k * ROWS, stations), here]
            send_ref[pl.ds(k * stations, stations), :] = lag_ref[pl.ds(k * ROWS, stations), there]

    small = (slots * stations * stations, half)
    return call(
        body,
        [((rows, 2 * freqs), BF16), (small, F32), (small, F32)],
        [*blocks, kernel],
        "forward",
        [pltpu.VMEM((count, 2 * segs, ROWS, freqs), F32), pltpu.VMEM((rows, lags), F32)],
        [table, place, seg],
    )


def misfit(a, b, observed, table, place, seg, scale):
    slots, stations, _, lags = observed.shape
    half = lags // 2

    def body(table_ref, place_ref, seg_ref, a_ref, b_ref, obs_ref, o_ref):
        here = pl.ds(pl.multiple_of((seg_ref[0] & 1) * half, 128), half)
        column = lax.broadcasted_iota(jnp.int32, (stations, half), 0)
        pad = jnp.zeros((ROWS - stations, half), F32)
        for r in range(slots):
            p, q = table_ref[0, r], table_ref[1, r]
            low = jnp.where(p < 0, stations, jnp.where(p != q, -1, 0))
            same = jnp.where(p == q, 1, 0)
            tiles = []
            for row in range(stations):
                at = pl.ds((r * stations + row) * stations, stations)
                value = jnp.tanh(scale * (a_ref[at, :] + b_ref[at, :]) - obs_ref[r, row, :, here])
                value = jnp.where(column > low + same * row, value, 0.0)
                tiles += [value, pad]
            for row in range(0, stations, 2):
                at = pl.ds((r * stations + row) * ROWS, 2 * ROWS)
                o_ref[at, :] = jnp.concatenate(tiles[2 * row : 2 * row + 4], axis=0).astype(BF16)

    return call(body, ((slots * stations * ROWS, half), BF16), [a, b, observed], "misfit", (), [table, place, seg])


def backward(mine, other, cross, kernel, table, place, seg, slots, stations, blocks, scale):
    rows, half = mine.shape
    freqs = kernel.shape[0] // 2
    lane = 256
    outer = blocks // 2
    targets = blocks * stations
    part = outer * stations

    def body(table_ref, place_ref, seg_ref, mine_ref, other_ref, cross_ref, k_ref, keep_ref, send_ref):
        own = place_ref[0]
        m = lax.broadcasted_iota(jnp.int32, (targets, rows), 0)
        n = m % stations
        group = m // stations
        block = 2 * ((own // 2 + group % outer) % outer) + ((own % 2) ^ (group // outer))
        k = lax.broadcasted_iota(jnp.int32, (targets, rows), 1)
        b = k % ROWS
        a = (k // ROWS) % stations
        r = k // (ROWS * stations)
        first = jnp.full((targets, rows), -1, jnp.int32)
        second = jnp.full((targets, rows), -1, jnp.int32)
        for s in range(slots):
            first = jnp.where(r == s, table_ref[0, s], first)
            second = jnp.where(r == s, table_ref[1, s], second)
        left = jnp.where((first == block) & (a == n), 1.0, 0.0)
        right = jnp.where((second == block) & (b == n), 1.0, 0.0)
        plus = (left + right).astype(BF16)
        minus = (left - right).astype(BF16)
        here = pl.ds(pl.multiple_of((seg_ref[0] & 1) * half, 128), half)
        there = pl.ds(pl.multiple_of((1 - (seg_ref[0] & 1)) * half, 128), half)
        res_mine = mine_ref[...]
        res_other = other_ref[...]
        contract = (((1,), (1,)), ((), ()))

        def gamma(at):
            one = lax.dot_general(res_mine, k_ref[at, here], contract, preferred_element_type=F32)
            two = lax.dot_general(res_other, k_ref[at, there], contract, preferred_element_type=F32)
            return scale * (one + two)

        def total(select, value):
            high = value.astype(BF16)
            rest = value - high.astype(F32)
            middle = rest.astype(BF16)
            low = (rest - middle.astype(F32)).astype(BF16)
            out = jnp.dot(select, high, preferred_element_type=F32)
            out = out + jnp.dot(select, middle, preferred_element_type=F32)
            return out + jnp.dot(select, low, preferred_element_type=F32)

        for f in range(0, freqs, lane):
            real = gamma(pl.ds(f, lane))
            imag = gamma(pl.ds(freqs + f, lane))
            stack_real = cross_ref[:, pl.ds(f, lane)].astype(F32)
            stack_imag = cross_ref[:, pl.ds(freqs + f, lane)].astype(F32)
            common = total(plus, real * stack_real + imag * stack_imag)
            twist = total(minus, imag * stack_real - real * stack_imag)
            into = keep_ref if f < freqs // 2 else send_ref
            at = pl.ds(f % (freqs // 2), lane)
            for y in range(2):
                into[pl.ds((2 * y) * part, part), at] = common[y * part : (y + 1) * part]
                into[pl.ds((2 * y + 1) * part, part), at] = twist[y * part : (y + 1) * part]

    shape = ((2 * targets, freqs // 2), F32)
    return call(body, [shape, shape], [mine, other, cross, kernel], "backward", (), [table, place, seg])


def add_split(a, b, axis):
    half = a.shape[axis] // 2
    parts = [lax.slice_in_dim(a, k, k + half, axis=axis) + lax.slice_in_dim(b, k, k + half, axis=axis) for k in (0, half)]
    return parts


def add_split_blocks(a, b, stations):
    rows, width = a.shape
    count = rows // (2 * stations)

    def body(a_ref, b_ref, *out_refs):
        for d in range(count):
            for c in range(2):
                at = pl.ds((c * count + d) * stations, stations)
                out_refs[d][c] = a_ref[at, :] + b_ref[at, :]

    return call(body, [((2, stations, width), F32)] * count, [a, b], "add_split_blocks")


def finish(pieces):
    _, stations, width = pieces[0].shape

    def body(*refs):
        o_ref = refs[-1]
        for c in range(2):
            value = refs[0][c]
            for ref in refs[1:-1]:
                value = value + ref[c]
            for n in range(stations):
                o_ref[n, pl.ds(c, 1), :] = value[n : n + 1]

    return call(body, ((stations, 2, width), F32), pieces, "finish", inside=False)


def on_device(spectra, observed, pair_table):
    stations, segs, _, freqs = spectra.shape
    slots = pair_table.shape[0]
    lags = observed.shape[3]
    sta_devices = lax.axis_size("sta")
    seg_devices = lax.axis_size("seg")
    bits = seg_devices.bit_length() - 1
    scale = 1.0 / math.sqrt(freqs * segs * seg_devices)
    seg = lax.axis_index("seg").astype(jnp.int32)
    sta = lax.axis_index("sta").astype(jnp.int32)
    seg_at = seg.reshape(1)
    place = sta.reshape(1)
    table = pair_table.T

    block = prepare(spectra, seg_at, seg_devices)
    def sx(v, d):
        return swap(v, "sta", sta_devices, d)
    top = sta_devices // 2
    far = sx(block, top)
    moved = {0: block, top: far}
    for e in range(1, top):
        moved[e] = sx(block, e)
    for e in range(1, top):
        moved[top + e] = sx(far, e)
    order = [0, top, *range(1, top), *range(top + 1, sta_devices)]
    blocks = [moved[d] for d in order]
    kernel = lag_kernel(freqs, lags, seg_at, seg_devices)
    cross, mine, send = forward(blocks, order, kernel, table, place, seg_at, segs, stations, slots)
    total = mine + swap(send, "seg", seg_devices, 1)
    for b in range(1, bits - 1):
        total = total + swap(total, "seg", seg_devices, 1 << b)
    last = swap(total, "seg", seg_devices, 1 << (bits - 1))
    residual = misfit(total, last, observed, table, place, seg_at, scale)
    other = swap(residual, "seg", seg_devices, 1)
    keep, send = backward(
        residual, other, cross, kernel, table, place, seg_at, slots, stations, sta_devices, scale
    )
    for b in range(bits - 1):
        keep, send = add_split(keep, swap(send, "seg", seg_devices, 1 << b), 1)
    keep, send = add_split(keep, swap(send, "seg", seg_devices, 1 << (bits - 1)), 0)
    pieces = add_split_blocks(keep, swap(send, "sta", sta_devices, 1), stations)
    arrived = [shift(piece, "sta", sta_devices, 2 * d) for d, piece in enumerate(pieces) if d]
    return finish([pieces[0], *arrived])


def solution(mesh):
    placed = (P("sta", "seg", None, None), P("sta", None, None, None), P("sta", None))
    return jax.shard_map(
        on_device, mesh=mesh, in_specs=placed, out_specs=P("sta", None, "seg"), check_vma=False
    )
```

```python
import math

import jax
import jax.numpy as jnp
from jax import lax
from jax.experimental import pallas as pl
from jax.experimental.pallas import tpu as pltpu
from jax.sharding import PartitionSpec as P

ROWS = 8

F32 = jnp.float32
BF16 = jnp.bfloat16


def call(body, outs, operands, name, scratch=(), scalars=(), inside=True, limit=24 << 20):
    smem = pl.BlockSpec(memory_space=pltpu.SMEM)
    vmem = pl.BlockSpec(memory_space=pltpu.VMEM)
    operands = [pltpu.with_memory_space_constraint(x, pltpu.VMEM) for x in operands]
    single = isinstance(outs, tuple)
    out_list = [outs] if single else outs
    result = pl.pallas_call(
        body,
        out_shape=[pltpu.VMEM(s, d) if inside else jax.ShapeDtypeStruct(s, d) for s, d in out_list],
        in_specs=[smem] * len(scalars) + [vmem] * len(operands),
        out_specs=[vmem] * len(out_list),
        scratch_shapes=list(scratch),
        name=name,
        compiler_params=pltpu.CompilerParams(vmem_limit_bytes=limit),
    )(*scalars, *operands)
    return result[0] if single else result


def reverse_bits(value, bits):
    out = 0
    for b in range(bits):
        out |= ((value >> b) & 1) << (bits - 1 - b)
    return out


def shift(x, axis, size, step):
    return lax.ppermute(x, axis, [(i, (i + step) % size) for i in range(size)])


def swap(x, axis, size, bit):
    return lax.ppermute(x, axis, [(i, i ^ bit) for i in range(size)])


def prepare(spectra, seg, seg_devices):
    stations, segs, parts, freqs = spectra.shape
    bits = seg_devices.bit_length() - 1
    width = freqs // seg_devices
    order = [reverse_bits(k, bits) for k in range(seg_devices)]
    aligned = width % 128 == 0
    if not aligned:
        chunks = spectra.reshape(stations, segs, parts, seg_devices, width)
        spectra = jnp.take(chunks, jnp.array(order) ^ seg[0], axis=3).reshape(spectra.shape)

    def body(seg_ref, x_ref, o_ref, tmp):
        for n in range(stations):
            for t in range(segs):
                value = x_ref[n, t].astype(F32)
                for c in range(parts):
                    tmp[pl.ds((t * parts + c) * stations + n, 1), :] = value[c : c + 1]
        for k in range(seg_devices):
            to = pl.ds(k * width, width)
            if aligned:
                at = pl.ds(pl.multiple_of((seg_ref[0] ^ order[k]) * width, 128), width)
            else:
                at = to
            o_ref[:, to] = tmp[:, at].astype(BF16)

    rows = segs * parts * stations
    return call(body, ((rows, freqs), BF16), [spectra], "prepare", [pltpu.VMEM((rows, freqs), F32)], [seg])


def lag_kernel(freqs, lags, seg, seg_devices):
    bits = seg_devices.bit_length() - 1
    width = freqs // seg_devices
    order = [reverse_bits(k, bits) for k in range(seg_devices)]
    fine = math.gcd(width, 64)
    coarse = freqs // fine
    period = 2 * freqs

    def body(seg_ref, o_ref, cos_ref, sin_ref):
        def table(count, step):
            f = lax.broadcasted_iota(jnp.int32, (count, lags), 0) * step
            offset = lax.broadcasted_iota(jnp.int32, (count, lags), 1) - lags // 2
            phase = (f * offset) & (period - 1)
            angle = math.pi / freqs * phase.astype(F32)
            return jnp.cos(angle), jnp.sin(angle)

        fine_cos, fine_sin = table(fine, 1)
        big_cos, big_sin = table(coarse, fine)
        cos_ref[...] = big_cos
        sin_ref[...] = big_sin
        for k in range(seg_devices):
            for s in range(width // fine):
                row = (seg_ref[0] ^ order[k]) * (width // fine) + s
                c = cos_ref[pl.ds(row, 1), :]
                d = sin_ref[pl.ds(row, 1), :]
                at = k * width + s * fine
                o_ref[pl.ds(at, fine), :] = (fine_cos * c - fine_sin * d).astype(BF16)
                o_ref[pl.ds(freqs + at, fine), :] = (-(fine_sin * c + fine_cos * d)).astype(BF16)

    return call(
        body,
        ((2 * freqs, lags), BF16),
        [],
        "lag_kernel",
        [pltpu.VMEM((coarse, lags), F32)] * 2,
        [seg],
    )


def forward(blocks, order, kernel, table, place, seg, segs, stations, slots):
    count = len(blocks)
    freqs = blocks[0].shape[1]
    lags = kernel.shape[1]
    half = lags // 2
    rows = slots * stations * ROWS
    lane = 256

    def body(table_ref, place_ref, seg_ref, *refs):
        block_refs = refs[:count]
        k_ref, cross_ref, send_ref, x_ref, lag_ref = refs[count:]
        own = place_ref[0]
        pad = jnp.zeros((ROWS - stations, freqs), F32)
        for k, d in enumerate(order):
            at = own ^ d
            value = block_refs[k][...].astype(F32)
            for r in range(2 * segs):
                x_ref[at, r] = jnp.concatenate([value[r * stations : (r + 1) * stations], pad], axis=0)

        def one_slot(r, carry):
            p = jnp.maximum(table_ref[0, r], 0)
            q = jnp.maximum(table_ref[1, r], 0)
            for f in range(0, freqs, lane):
                fs = pl.ds(f, lane)
                right = [x_ref[q, k, :, fs] for k in range(2 * segs)]
                real, imag = [], []
                for a in range(stations):
                    re = im = None
                    for t in range(segs):
                        x0 = x_ref[p, 2 * t, pl.ds(a, 1), fs]
                        x1 = x_ref[p, 2 * t + 1, pl.ds(a, 1), fs]
                        y0, y1 = right[2 * t], right[2 * t + 1]
                        u = x0 * y0 + x1 * y1
                        v = x1 * y0 - x0 * y1
                        re = u if re is None else re + u
                        im = v if im is None else im + v
                    real.append(re)
                    imag.append(im)
                for a in range(0, stations, 2):
                    at = pl.multiple_of((r * stations + a) * ROWS, 2 * ROWS)
                    cross_ref[pl.ds(at, 2 * ROWS), fs] = jnp.concatenate(real[a : a + 2], axis=0).astype(BF16)
                    cross_ref[pl.ds(at, 2 * ROWS), pl.ds(freqs + f, lane)] = jnp.concatenate(
                        imag[a : a + 2], axis=0
                    ).astype(BF16)
            return carry

        lax.fori_loop(0, slots, one_slot, 0)
        lag_terms(1 - (seg_ref[0] & 1), cross_ref, k_ref, send_ref, lag_ref, slots * stations, stations)

    small = (slots * stations * stations, half)
    return call(
        body,
        [((rows, 2 * freqs), BF16), (small, F32)],
        [*blocks, kernel],
        "forward",
        [pltpu.VMEM((count, 2 * segs, ROWS, freqs), F32), pltpu.VMEM((rows, half), F32)],
        [table, place, seg],
    )


def lag_terms(core, cross_ref, k_ref, out_ref, lag_ref, tiles, stations):
    half = k_ref.shape[1] // 2
    here = pl.ds(pl.multiple_of(core * half, 128), half)
    lag_ref[...] = jnp.dot(cross_ref[...], k_ref[:, here], preferred_element_type=F32)
    for k in range(tiles):
        out_ref[pl.ds(k * stations, stations), :] = lag_ref[pl.ds(k * ROWS, stations), :]


def forward_own(cross, kernel, seg, tiles, stations):
    half = kernel.shape[1] // 2

    def body(seg_ref, cross_ref, k_ref, o_ref, lag_ref):
        lag_terms(seg_ref[0] & 1, cross_ref, k_ref, o_ref, lag_ref, tiles, stations)

    return call(
        body,
        ((tiles * stations, half), F32),
        [cross, kernel],
        "forward_own",
        [pltpu.VMEM((cross.shape[0], half), F32)],
        [seg],
    )


def misfit(a, b, observed, table, place, seg, scale):
    slots, stations, _, lags = observed.shape
    half = lags // 2

    def body(table_ref, place_ref, seg_ref, a_ref, b_ref, obs_ref, o_ref):
        here = pl.ds(pl.multiple_of((seg_ref[0] & 1) * half, 128), half)
        column = lax.broadcasted_iota(jnp.int32, (stations, half), 0)
        pad = jnp.zeros((ROWS - stations, half), F32)
        for r in range(slots):
            p, q = table_ref[0, r], table_ref[1, r]
            low = jnp.where(p < 0, stations, jnp.where(p != q, -1, 0))
            same = jnp.where(p == q, 1, 0)
            tiles = []
            for row in range(stations):
                at = pl.ds((r * stations + row) * stations, stations)
                value = jnp.tanh(scale * (a_ref[at, :] + b_ref[at, :]) - obs_ref[r, row, :, here])
                value = jnp.where(column > low + same * row, value, 0.0)
                tiles += [value, pad]
            for row in range(0, stations, 2):
                at = pl.ds((r * stations + row) * ROWS, 2 * ROWS)
                o_ref[at, :] = jnp.concatenate(tiles[2 * row : 2 * row + 4], axis=0).astype(BF16)

    return call(body, ((slots * stations * ROWS, half), BF16), [a, b, observed], "misfit", (), [table, place, seg])


def gamma_terms(residual, kernel, seg, core, name, base=None):
    rows, half = residual.shape
    depth = kernel.shape[0]
    contract = (((1,), (1,)), ((), ()))

    def body(seg_ref, r_ref, k_ref, o_ref):
        here = pl.ds(pl.multiple_of((seg_ref[0] & 1 ^ core) * half, 128), half)
        o_ref[...] = lax.dot_general(r_ref[...], k_ref[:, here], contract, preferred_element_type=F32)

    return call(body, ((rows, depth), F32), [residual, kernel], name, (), [seg])


def backward(base, other, cross, kernel, table, place, seg, slots, stations, blocks, scale, part):
    rows, half = other.shape
    freqs = kernel.shape[0] // 2
    lane = min(256, freqs // 2)
    outer = blocks // 2
    targets = blocks * stations
    group_rows = outer * stations
    begin = part * (freqs // 2)

    def body(table_ref, place_ref, seg_ref, base_ref, other_ref, cross_ref, k_ref, o_ref):
        own = place_ref[0]
        m = lax.broadcasted_iota(jnp.int32, (targets, rows), 0)
        n = m % stations
        group = m // stations
        block = 2 * ((own // 2 + group % outer) % outer) + ((own % 2) ^ (group // outer))
        k = lax.broadcasted_iota(jnp.int32, (targets, rows), 1)
        b = k % ROWS
        a = (k // ROWS) % stations
        r = k // (ROWS * stations)
        first = jnp.full((targets, rows), -1, jnp.int32)
        second = jnp.full((targets, rows), -1, jnp.int32)
        for s in range(slots):
            first = jnp.where(r == s, table_ref[0, s], first)
            second = jnp.where(r == s, table_ref[1, s], second)
        left = jnp.where((first == block) & (a == n), 1.0, 0.0)
        right = jnp.where((second == block) & (b == n), 1.0, 0.0)
        plus = (left + right).astype(BF16)
        minus = (left - right).astype(BF16)
        there = pl.ds(pl.multiple_of((1 - (seg_ref[0] & 1)) * half, 128), half)
        residual = other_ref[...]
        contract = (((1,), (1,)), ((), ()))

        def gamma(at):
            rest = lax.dot_general(residual, k_ref[at, there], contract, preferred_element_type=F32)
            return scale * (base_ref[:, at] + rest)

        def total(select, value):
            high = value.astype(BF16)
            rest = value - high.astype(F32)
            middle = rest.astype(BF16)
            low = (rest - middle.astype(F32)).astype(BF16)
            out = jnp.dot(select, high, preferred_element_type=F32)
            out = out + jnp.dot(select, middle, preferred_element_type=F32)
            return out + jnp.dot(select, low, preferred_element_type=F32)

        for f in range(0, freqs // 2, lane):
            real = gamma(pl.ds(begin + f, lane))
            imag = gamma(pl.ds(freqs + begin + f, lane))
            stack_real = cross_ref[:, pl.ds(begin + f, lane)].astype(F32)
            stack_imag = cross_ref[:, pl.ds(freqs + begin + f, lane)].astype(F32)
            common = total(plus, real * stack_real + imag * stack_imag)
            twist = total(minus, imag * stack_real - real * stack_imag)
            at = pl.ds(f, lane)
            for y in range(2):
                o_ref[pl.ds((2 * y) * group_rows, group_rows), at] = common[y * group_rows : (y + 1) * group_rows]
                o_ref[pl.ds((2 * y + 1) * group_rows, group_rows), at] = twist[y * group_rows : (y + 1) * group_rows]

    name = ("backward_own", "backward_mate")[part]
    return call(
        body, ((2 * targets, freqs // 2), F32), [base, other, cross, kernel], name, (), [table, place, seg]
    )


def add_split(a, b, axis):
    half = a.shape[axis] // 2
    parts = [lax.slice_in_dim(a, k, k + half, axis=axis) + lax.slice_in_dim(b, k, k + half, axis=axis) for k in (0, half)]
    return parts


def add_quarters(a, b):
    rows, width = a.shape
    high, wide = rows // 2, width // 2

    def body(a_ref, b_ref, *out_refs):
        for k, ref in enumerate(out_refs):
            at = pl.ds((k >> 1) * high, high), pl.ds((k & 1) * wide, wide)
            ref[...] = a_ref[at] + b_ref[at]

    return call(body, [((high, wide), F32)] * 4, [a, b], "add_quarters")


def sum_blocks(arrays, stations):
    rows, width = arrays[0].shape
    count = rows // (2 * stations)
    terms = len(arrays)

    def body(*refs):
        for d in range(count):
            for c in range(2):
                at = pl.ds((c * count + d) * stations, stations)
                value = refs[0][at, :]
                for ref in refs[1:terms]:
                    value = value + ref[at, :]
                refs[terms + d][c] = value

    return call(body, [((2, stations, width), F32)] * count, arrays, "sum_blocks")


def finish(pieces):
    _, stations, width = pieces[0].shape

    def body(*refs):
        o_ref = refs[-1]
        for c in range(2):
            value = refs[0][c]
            for ref in refs[1:-1]:
                value = value + ref[c]
            for n in range(stations):
                o_ref[n, pl.ds(c, 1), :] = value[n : n + 1]

    return call(body, ((stations, 2, width), F32), pieces, "finish", inside=False)


def on_device(spectra, observed, pair_table):
    stations, segs, _, freqs = spectra.shape
    slots = pair_table.shape[0]
    lags = observed.shape[3]
    sta_devices = lax.axis_size("sta")
    seg_devices = lax.axis_size("seg")
    bits = seg_devices.bit_length() - 1
    scale = 1.0 / math.sqrt(freqs * segs * seg_devices)
    seg = lax.axis_index("seg").astype(jnp.int32)
    sta = lax.axis_index("sta").astype(jnp.int32)
    seg_at = seg.reshape(1)
    place = sta.reshape(1)
    table = pair_table.T

    block = prepare(spectra, seg_at, seg_devices)
    def sx(v, d):
        return swap(v, "sta", sta_devices, d)
    top = sta_devices // 2
    far = sx(block, top)
    moved = {0: block, top: far}
    for e in range(1, top):
        moved[e] = sx(block, e)
    for e in range(1, top):
        moved[top + e] = sx(far, e)
    order = [0, top, *range(1, top), *range(top + 1, sta_devices)]
    blocks = [moved[d] for d in order]
    kernel = lag_kernel(freqs, lags, seg_at, seg_devices)
    cross, send = forward(blocks, order, kernel, table, place, seg_at, segs, stations, slots)
    sent = swap(send, "seg", seg_devices, 1)
    total = forward_own(cross, kernel, seg_at, slots * stations, stations) + sent
    for b in range(1, bits - 1):
        total = total + swap(total, "seg", seg_devices, 1 << b)
    last = swap(total, "seg", seg_devices, 1 << (bits - 1))
    residual = misfit(total, last, observed, table, place, seg_at, scale)
    other = swap(residual, "seg", seg_devices, 1)
    base = gamma_terms(residual, kernel, seg_at, 0, "gamma_own")
    rest = (base, other, cross, kernel, table, place, seg_at, slots, stations, sta_devices, scale)
    send = swap(backward(*rest, 1), "seg", seg_devices, 1)
    keep = backward(*rest, 0)
    for b in range(1, bits - 1):
        keep, out = add_split(keep, send, 1)
        send = swap(out, "seg", seg_devices, 1 << b)
    own, x, y, xy = add_quarters(keep, send)
    top = 1 << (bits - 1)
    corner = [
        (i * seg_devices + j, (i ^ 1) * seg_devices + (j ^ top))
        for i in range(sta_devices)
        for j in range(seg_devices)
    ]
    arrays = [
        own,
        swap(x, "seg", seg_devices, top),
        swap(y, "sta", sta_devices, 1),
        lax.ppermute(xy, ("sta", "seg"), corner),
    ]
    pieces = sum_blocks(arrays, stations)
    arrived = [shift(piece, "sta", sta_devices, 2 * d) for d, piece in enumerate(pieces) if d]
    return finish([pieces[0], *arrived])


def solution(mesh):
    placed = (P("sta", "seg", None, None), P("sta", None, None, None), P("sta", None))
    return jax.shard_map(
        on_device, mesh=mesh, in_specs=placed, out_specs=P("sta", None, "seg"), check_vma=False
    )
```

```python
import math

import jax
import jax.numpy as jnp
from jax import lax
from jax.experimental import pallas as pl
from jax.experimental.pallas import tpu as pltpu
from jax.sharding import PartitionSpec as P

ROWS = 8

F32 = jnp.float32
BF16 = jnp.bfloat16


def call(body, outs, operands, name, scratch=(), scalars=(), inside=True, limit=24 << 20):
    smem = pl.BlockSpec(memory_space=pltpu.SMEM)
    vmem = pl.BlockSpec(memory_space=pltpu.VMEM)
    operands = [pltpu.with_memory_space_constraint(x, pltpu.VMEM) for x in operands]
    single = isinstance(outs, tuple)
    out_list = [outs] if single else outs
    result = pl.pallas_call(
        body,
        out_shape=[pltpu.VMEM(s, d) if inside else jax.ShapeDtypeStruct(s, d) for s, d in out_list],
        in_specs=[smem] * len(scalars) + [vmem] * len(operands),
        out_specs=[vmem] * len(out_list),
        scratch_shapes=list(scratch),
        name=name,
        compiler_params=pltpu.CompilerParams(vmem_limit_bytes=limit),
    )(*scalars, *operands)
    return result[0] if single else result


def swap(x, axes, sizes, bits):
    places = [()]
    for size in sizes:
        places = [place + (i,) for place in places for i in range(size)]

    def flat(place):
        out = 0
        for i, size in zip(place, sizes):
            out = out * size + i
        return out

    pairs = [(flat(p), flat(tuple(i ^ b for i, b in zip(p, bits)))) for p in places]
    return lax.ppermute(x, axes if len(axes) > 1 else axes[0], pairs)


def prepare(spectra, seg, seg_devices):
    stations, segs, parts, freqs = spectra.shape
    width = freqs // seg_devices
    aligned = width % 128 == 0
    if not aligned:
        chunks = spectra.reshape(stations, segs, parts, seg_devices, width)
        spectra = jnp.take(chunks, jnp.arange(seg_devices) ^ seg[0], axis=3).reshape(spectra.shape)
    rows = segs * parts * stations

    def body(seg_ref, x_ref, *refs):
        tmp = refs[-1]
        for n in range(stations):
            for t in range(segs):
                tmp[pl.ds((n * segs + t) * parts, parts), :] = x_ref[n, t].astype(F32)
        for k in range(seg_devices):
            at = pl.ds(k * width, width)
            if aligned:
                at = pl.ds(pl.multiple_of((seg_ref[0] ^ k) * width, 128), width)
            refs[k // 2][:, pl.ds(k % 2 * width, width)] = tmp[:, at].astype(BF16)

    outs = [((rows, 2 * width), BF16)] * (seg_devices // 2)
    return call(body, outs, [spectra], "prepare", [pltpu.VMEM((rows, freqs), F32)], [seg])


def pack(arrays, name):
    rows, width = arrays[0].shape

    def body(*refs):
        for k, ref in enumerate(refs[:-1]):
            refs[-1][pl.ds(k * rows, rows), :] = ref[...]

    return call(body, ((len(arrays) * rows, width), arrays[0].dtype), arrays, name)


def lag_kernel(freqs, lags, seg, seg_devices):
    width = freqs // seg_devices
    fine = math.gcd(width, 64)
    coarse = freqs // fine
    period = 2 * freqs

    def body(seg_ref, o_ref, cos_ref, sin_ref):
        def table(count, step):
            f = lax.broadcasted_iota(jnp.int32, (count, lags), 0) * step
            offset = lax.broadcasted_iota(jnp.int32, (count, lags), 1) - lags // 2
            phase = (f * offset) & (period - 1)
            angle = math.pi / freqs * phase.astype(F32)
            return jnp.cos(angle), jnp.sin(angle)

        fine_cos, fine_sin = table(fine, 1)
        big_cos, big_sin = table(coarse, fine)
        cos_ref[...] = big_cos
        sin_ref[...] = big_sin
        for k in range(2):
            for s in range(width // fine):
                row = (seg_ref[0] ^ k) * (width // fine) + s
                c = cos_ref[pl.ds(row, 1), :]
                d = sin_ref[pl.ds(row, 1), :]
                at = k * width + s * fine
                o_ref[pl.ds(at, fine), :] = (fine_cos * c - fine_sin * d).astype(BF16)
                o_ref[pl.ds(2 * width + at, fine), :] = (-(fine_sin * c + fine_cos * d)).astype(BF16)

    scratch = [pltpu.VMEM((coarse, lags), F32)] * 2
    return call(body, ((4 * width, lags), BF16), [], "lag_kernel", scratch, [seg])


def selection(table, sta, slots, stations, blocks):
    rows = slots * stations * ROWS
    targets = blocks * stations
    outer = blocks // 2

    def body(table_ref, sta_ref, plus_ref, minus_ref):
        m = lax.broadcasted_iota(jnp.int32, (targets, rows), 0)
        n = m % stations
        group = m // stations
        block = sta_ref[0] ^ (2 * (group % outer) + group // outer)
        k = lax.broadcasted_iota(jnp.int32, (targets, rows), 1)
        b = k % ROWS
        a = (k // ROWS) % stations
        r = k // (ROWS * stations)
        first = jnp.full((targets, rows), -1, jnp.int32)
        second = jnp.full((targets, rows), -1, jnp.int32)
        for s in range(slots):
            first = jnp.where(r == s, table_ref[0, s], first)
            second = jnp.where(r == s, table_ref[1, s], second)
        left = jnp.where((first == block) & (a == n), 1.0, 0.0)
        right = jnp.where((second == block) & (b == n), 1.0, 0.0)
        plus_ref[...] = (left + right).astype(BF16)
        minus_ref[...] = (left - right).astype(BF16)

    return call(body, [((targets, rows), BF16)] * 2, [], "selection", (), [table, sta])


def forward(blocks, order, kernel, table, sta, seg, groups, segs, stations, slots):
    count = len(blocks)
    height, width = blocks[0].shape
    group_rows = height // groups
    half = kernel.shape[1] // 2
    rows = slots * stations * ROWS
    lane = 128
    step = 2 * segs
    spare = (ROWS - stations) * step

    def body(table_ref, sta_ref, seg_ref, *refs):
        k_ref, cross_ref, send_ref, x_ref, lag_ref = refs[count:]
        for k, d in enumerate(order):
            at = sta_ref[0] ^ d
            for i in range(width // lane):
                x_ref[at, i, pl.ds(0, height), :] = refs[k][:, pl.ds(i * lane, lane)].astype(F32)
                x_ref[at, i, pl.ds(height, spare), :] = jnp.zeros((spare, lane), F32)

        def one_slot(r, carry):
            p = jnp.maximum(table_ref[0, r], 0)
            q = jnp.maximum(table_ref[1, r], 0)
            for g in range(groups):
                for i in range(width // lane):
                    right = [x_ref[q, i, pl.ds(g * group_rows + k, ROWS, stride=step), :] for k in range(step)]
                    real, imag = [], []
                    for a in range(stations):
                        re = im = None
                        for t in range(segs):
                            at = g * group_rows + a * step + 2 * t
                            x0 = x_ref[p, i, pl.ds(at, 1), :]
                            x1 = x_ref[p, i, pl.ds(at + 1, 1), :]
                            y0, y1 = right[2 * t], right[2 * t + 1]
                            u = x0 * y0 + x1 * y1
                            v = x1 * y0 - x0 * y1
                            re = u if re is None else re + u
                            im = v if im is None else im + v
                        real.append(re)
                        imag.append(im)
                    for a in range(0, stations, 2):
                        at = pl.multiple_of(g * rows + (r * stations + a) * ROWS, 2 * ROWS)
                        at = pl.ds(at, 2 * ROWS)
                        cross_ref[at, pl.ds(i * lane, lane)] = jnp.concatenate(real[a : a + 2], axis=0).astype(BF16)
                        cross_ref[at, pl.ds(width + i * lane, lane)] = jnp.concatenate(imag[a : a + 2], axis=0).astype(BF16)
            return carry

        lax.fori_loop(0, slots, one_slot, 0)
        lag_terms(1 - (seg_ref[0] & 1), cross_ref, k_ref, send_ref, lag_ref, groups, stations)

    return call(
        body,
        [((groups * rows, 2 * width), BF16), ((slots * stations * stations, half), F32)],
        [*blocks, kernel],
        "forward",
        [pltpu.VMEM((count, width // lane, height + spare, lane), F32), pltpu.VMEM((groups * rows, half), F32)],
        [table, sta, seg],
    )


def lag_terms(core, cross_ref, k_ref, out_ref, lag_ref, groups, stations):
    half = k_ref.shape[1] // 2
    here = pl.ds(pl.multiple_of(core * half, 128), half)
    lag_ref[...] = jnp.dot(cross_ref[...], k_ref[:, here], preferred_element_type=F32)
    rows = lag_ref.shape[0] // groups
    for k in range(rows // ROWS):
        value = lag_ref[pl.ds(k * ROWS, stations), :]
        for g in range(1, groups):
            value = value + lag_ref[pl.ds(g * rows + k * ROWS, stations), :]
        out_ref[pl.ds(k * stations, stations), :] = value


def forward_own(cross, kernel, seg, groups, stations):
    half = kernel.shape[1] // 2
    tiles = cross.shape[0] // (groups * ROWS)

    def body(seg_ref, cross_ref, k_ref, o_ref, lag_ref):
        lag_terms(seg_ref[0] & 1, cross_ref, k_ref, o_ref, lag_ref, groups, stations)

    scratch = [pltpu.VMEM((cross.shape[0], half), F32)]
    return call(body, ((tiles * stations, half), F32), [cross, kernel], "forward_own", scratch, [seg])


def misfit(a, b, observed, table, place, seg, scale):
    slots, stations, _, lags = observed.shape
    half = lags // 2

    def body(table_ref, place_ref, seg_ref, a_ref, b_ref, obs_ref, o_ref):
        here = pl.ds(pl.multiple_of((seg_ref[0] & 1) * half, 128), half)
        column = lax.broadcasted_iota(jnp.int32, (stations, half), 0)
        pad = jnp.zeros((ROWS - stations, half), F32)
        for r in range(slots):
            p, q = table_ref[0, r], table_ref[1, r]
            low = jnp.where(p < 0, stations, jnp.where(p != q, -1, 0))
            same = jnp.where(p == q, 1, 0)
            tiles = []
            for row in range(stations):
                at = pl.ds((r * stations + row) * stations, stations)
                value = jnp.tanh(scale * (a_ref[at, :] + b_ref[at, :]) - obs_ref[r, row, :, here])
                value = jnp.where(column > low + same * row, value, 0.0)
                tiles += [value, pad]
            for row in range(0, stations, 2):
                at = pl.ds((r * stations + row) * ROWS, 2 * ROWS)
                o_ref[at, :] = jnp.concatenate(tiles[2 * row : 2 * row + 4], axis=0).astype(BF16)

    return call(body, ((slots * stations * ROWS, half), BF16), [a, b, observed], "misfit", (), [table, place, seg])


def gamma_terms(residual, kernel, seg, core, name):
    rows, half = residual.shape
    depth = kernel.shape[0]
    contract = (((1,), (1,)), ((), ()))

    def body(seg_ref, r_ref, k_ref, o_ref):
        here = pl.ds(pl.multiple_of((seg_ref[0] & 1 ^ core) * half, 128), half)
        o_ref[...] = lax.dot_general(r_ref[...], k_ref[:, here], contract, preferred_element_type=F32)

    return call(body, ((rows, depth), F32), [residual, kernel], name, (), [seg])


def backward(base, other, cross, kernel, plus, minus, seg, groups, stations, scale, part):
    rows, half = other.shape
    both = kernel.shape[0] // 2
    width = both // 2
    targets = plus.shape[0]
    group_rows = targets // 2
    begin = part * width

    def body(seg_ref, base_ref, other_ref, cross_ref, k_ref, plus_ref, minus_ref, o_ref):
        there = pl.ds(pl.multiple_of((1 - (seg_ref[0] & 1)) * half, 128), half)
        residual = other_ref[...]
        contract = (((1,), (1,)), ((), ()))

        def gamma(at):
            rest = lax.dot_general(residual, k_ref[at, there], contract, preferred_element_type=F32)
            return scale * (base_ref[:, at] + rest)

        def stack(at):
            value = cross_ref[pl.ds(0, rows), at].astype(F32)
            for g in range(1, groups):
                value = value + cross_ref[pl.ds(g * rows, rows), at].astype(F32)
            return value

        def total(select, value):
            high = value.astype(BF16)
            low = (value - high.astype(F32)).astype(BF16)
            return jnp.dot(select, high, preferred_element_type=F32) + jnp.dot(
                select, low, preferred_element_type=F32
            )

        real_at, imag_at = pl.ds(begin, width), pl.ds(both + begin, width)
        real, imag = gamma(real_at), gamma(imag_at)
        stack_real, stack_imag = stack(real_at), stack(imag_at)
        common = total(plus_ref[...], real * stack_real + imag * stack_imag)
        twist = total(minus_ref[...], imag * stack_real - real * stack_imag)
        for y in range(2):
            o_ref[pl.ds((2 * y) * group_rows, group_rows), :] = common[y * group_rows : (y + 1) * group_rows]
            o_ref[pl.ds((2 * y + 1) * group_rows, group_rows), :] = twist[y * group_rows : (y + 1) * group_rows]

    name = ("backward_own", "backward_mate")[part]
    operands = [base, other, cross, kernel, plus, minus]
    return call(body, ((2 * targets, width), F32), operands, name, (), [seg])


def add_split(a, b, axis):
    half = a.shape[axis] // 2
    parts = [lax.slice_in_dim(a, k, k + half, axis=axis) + lax.slice_in_dim(b, k, k + half, axis=axis) for k in (0, half)]
    return parts


def split_blocks(a, b, stations):
    rows, width = a.shape
    count = rows // (2 * stations)

    def body(a_ref, b_ref, *refs):
        for d in range(count):
            for c in range(2):
                at = pl.ds((c * count + d) * stations, stations)
                refs[d][c] = a_ref[at, :] + b_ref[at, :]

    return call(body, [((2, stations, width), F32)] * count, [a, b], "split_blocks")


def finish(pieces):
    _, stations, width = pieces[0].shape

    def body(*refs):
        o_ref = refs[-1]
        for c in range(2):
            value = refs[0][c]
            for ref in refs[1:-1]:
                value = value + ref[c]
            for n in range(stations):
                o_ref[n, pl.ds(c, 1), :] = value[n : n + 1]

    return call(body, ((stations, 2, width), F32), pieces, "finish", inside=False)


def on_device(spectra, observed, pair_table):
    stations, segs, _, freqs = spectra.shape
    slots = pair_table.shape[0]
    lags = observed.shape[3]
    stas = lax.axis_size("sta")
    seg_devices = lax.axis_size("seg")
    groups = seg_devices // 2
    scale = 1.0 / math.sqrt(freqs * segs * seg_devices)
    seg = lax.axis_index("seg").astype(jnp.int32).reshape(1)
    sta = lax.axis_index("sta").astype(jnp.int32).reshape(1)
    table = pair_table.T

    def along_sta(x, bit):
        return swap(x, ("sta",), (stas,), (bit,))

    def along_seg(x, bit):
        return swap(x, ("seg",), (seg_devices,), (bit,))

    top = stas // 2
    parts = prepare(spectra, seg, seg_devices)
    near = [parts[0]] + [along_seg(parts[h], 2 * h) for h in range(1, groups)]
    far = [
        swap(parts[h], ("sta", "seg"), (stas, seg_devices), (top, 2 * h)) if h else along_sta(parts[h], top)
        for h in range(groups)
    ]
    moved = {0: pack(near, "pack_near"), top: pack(far, "pack_far")}
    for e in range(1, top):
        moved[e] = along_sta(moved[0], e)
    for e in range(1, top):
        moved[top + e] = along_sta(moved[top], e)
    order = [0, top, *range(1, top), *range(top + 1, stas)]
    kernel = lag_kernel(freqs, lags, seg, seg_devices)
    plus, minus = selection(table, sta, slots, stations, stas)

    blocks = [moved[d] for d in order]
    blocks[0], kernel, plus, minus = lax.optimization_barrier((blocks[0], kernel, plus, minus))
    cross, send = forward(blocks, order, kernel, table, sta, seg, groups, segs, stations, slots)
    sent = along_seg(send, 1)
    total = forward_own(cross, kernel, seg, groups, stations) + sent
    bit = 2
    while 2 * bit < seg_devices:
        total = total + along_seg(total, bit)
        bit *= 2
    last = along_seg(total, bit)
    residual = misfit(total, last, observed, table, sta, seg, scale)
    other = along_seg(residual, 1)
    base = gamma_terms(residual, kernel, seg, 0, "gamma_own")
    rest = (base, other, cross, kernel, plus, minus, seg, groups, stations, scale)
    send = along_seg(backward(*rest, 1), 1)
    keep, send = add_split(backward(*rest, 0), send, 0)
    pieces = split_blocks(keep, along_sta(send, 1), stations)
    arrived = [along_sta(pieces[d], 2 * d) for d in (*range(2, top), 1)]
    return finish([pieces[0], *arrived])


def solution(mesh):
    placed = (P("sta", "seg", None, None), P("sta", None, None, None), P("sta", None))
    return jax.shard_map(
        on_device, mesh=mesh, in_specs=placed, out_specs=P("sta", None, "seg"), check_vma=False
    )
```

```python
import math

import jax
import jax.numpy as jnp
from jax import lax
from jax.experimental import pallas as pl
from jax.experimental.pallas import tpu as pltpu
from jax.sharding import PartitionSpec as P

ROWS = 8

F32 = jnp.float32
BF16 = jnp.bfloat16


def space(dtype):
    return pltpu.SMEM if dtype == jnp.int32 else pltpu.VMEM


def call(body, outs, operands, name, scratch=(), scalars=(), inside=True, limit=24 << 20):
    smem = pl.BlockSpec(memory_space=pltpu.SMEM)
    vmem = pl.BlockSpec(memory_space=pltpu.VMEM)
    operands = [pltpu.with_memory_space_constraint(x, pltpu.VMEM) for x in operands]
    single = isinstance(outs, tuple)
    out_list = [outs] if single else outs
    result = pl.pallas_call(
        body,
        out_shape=[space(d)(s, d) if inside else jax.ShapeDtypeStruct(s, d) for s, d in out_list],
        in_specs=[smem] * len(scalars) + [vmem] * len(operands),
        out_specs=[pl.BlockSpec(memory_space=space(d)) for _, d in out_list],
        scratch_shapes=list(scratch),
        name=name,
        compiler_params=pltpu.CompilerParams(vmem_limit_bytes=limit),
    )(*scalars, *operands)
    return result[0] if single else result


def swap(x, axes, sizes, bits):
    places = [()]
    for size in sizes:
        places = [place + (i,) for place in places for i in range(size)]

    def flat(place):
        out = 0
        for i, size in zip(place, sizes):
            out = out * size + i
        return out

    pairs = [(flat(p), flat(tuple(i ^ b for i, b in zip(p, bits)))) for p in places]
    return lax.ppermute(x, axes if len(axes) > 1 else axes[0], pairs)


def prepare(spectra, seg, seg_devices):
    stations, segs, parts, freqs = spectra.shape
    width = freqs // seg_devices
    aligned = width % 128 == 0
    if not aligned:
        chunks = spectra.reshape(stations, segs, parts, seg_devices, width)
        spectra = jnp.take(chunks, jnp.arange(seg_devices) ^ seg[0], axis=3).reshape(spectra.shape)
    rows = segs * parts * stations

    def body(seg_ref, x_ref, *refs):
        tmp = refs[-1]
        for n in range(stations):
            for t in range(segs):
                tmp[pl.ds((n * segs + t) * parts, parts), :] = x_ref[n, t].astype(F32)
        for k in range(seg_devices):
            at = pl.ds(k * width, width)
            if aligned:
                at = pl.ds(pl.multiple_of((seg_ref[0] ^ k) * width, 128), width)
            refs[k // 2][:, pl.ds(k % 2 * width, width)] = tmp[:, at].astype(BF16)

    outs = [((rows, 2 * width), BF16)] * (seg_devices // 2)
    return call(body, outs, [spectra], "prepare", [pltpu.VMEM((rows, freqs), F32)], [seg])


def pack(arrays, name):
    rows, width = arrays[0].shape

    def body(*refs):
        for k, ref in enumerate(refs[:-1]):
            refs[-1][pl.ds(k * rows, rows), :] = ref[...]

    return call(body, ((len(arrays) * rows, width), arrays[0].dtype), arrays, name)


def lag_kernel(freqs, lags, seg, seg_devices):
    width = freqs // seg_devices
    fine = math.gcd(width, 64)
    coarse = freqs // fine
    period = 2 * freqs

    def body(seg_ref, o_ref, cos_ref, sin_ref):
        def table(count, step):
            f = lax.broadcasted_iota(jnp.int32, (count, lags), 0) * step
            offset = lax.broadcasted_iota(jnp.int32, (count, lags), 1) - lags // 2
            phase = (f * offset) & (period - 1)
            angle = math.pi / freqs * phase.astype(F32)
            return jnp.cos(angle), jnp.sin(angle)

        fine_cos, fine_sin = table(fine, 1)
        big_cos, big_sin = table(coarse, fine)
        cos_ref[...] = big_cos
        sin_ref[...] = big_sin
        for k in range(2):
            for s in range(width // fine):
                row = (seg_ref[0] ^ k) * (width // fine) + s
                c = cos_ref[pl.ds(row, 1), :]
                d = sin_ref[pl.ds(row, 1), :]
                at = k * width + s * fine
                o_ref[pl.ds(at, fine), :] = (fine_cos * c - fine_sin * d).astype(BF16)
                o_ref[pl.ds(2 * width + at, fine), :] = (-(fine_sin * c + fine_cos * d)).astype(BF16)

    scratch = [pltpu.VMEM((coarse, lags), F32)] * 2
    return call(body, ((4 * width, lags), BF16), [], "lag_kernel", scratch, [seg])


def selection(table, sta, slots, stations, blocks):
    rows = slots * stations * ROWS
    targets = blocks * stations
    top = blocks // 2

    def body(table_ref, sta_ref, plus_ref, minus_ref, keep_ref):
        for i in range(2):
            for s in range(slots):
                keep_ref[i, s] = table_ref[i, s]
        m = lax.broadcasted_iota(jnp.int32, (targets, rows), 0)
        n = m % stations
        group = m // stations
        block = sta_ref[0] ^ (top * (group % 2) + group // 2)
        k = lax.broadcasted_iota(jnp.int32, (targets, rows), 1)
        b = k % ROWS
        a = (k // ROWS) % stations
        r = k // (ROWS * stations)
        first = jnp.full((targets, rows), -1, jnp.int32)
        second = jnp.full((targets, rows), -1, jnp.int32)
        for s in range(slots):
            first = jnp.where(r == s, table_ref[0, s], first)
            second = jnp.where(r == s, table_ref[1, s], second)
        left = jnp.where((first == block) & (a == n), 1.0, 0.0)
        right = jnp.where((second == block) & (b == n), 1.0, 0.0)
        plus_ref[...] = (left + right).astype(BF16)
        minus_ref[...] = (left - right).astype(BF16)

    outs = [((targets, rows), BF16), ((targets, rows), BF16), (table.shape, jnp.int32)]
    return call(body, outs, [], "selection", (), [table, sta])


def forward(blocks, order, kernel, table, sta, seg, groups, segs, stations, slots):
    count = len(blocks)
    height, width = blocks[0].shape
    group_rows = height // groups
    half = kernel.shape[1] // 2
    rows = slots * stations * ROWS
    lane = 128
    step = 2 * segs
    spare = (ROWS - stations) * step

    def body(table_ref, sta_ref, seg_ref, *refs):
        k_ref, cross_ref, send_ref, x_ref, lag_ref = refs[count:]
        for k, d in enumerate(order):
            at = sta_ref[0] ^ d
            for i in range(width // lane):
                x_ref[at, i, pl.ds(0, height), :] = refs[k][:, pl.ds(i * lane, lane)].astype(F32)
                x_ref[at, i, pl.ds(height, spare), :] = jnp.zeros((spare, lane), F32)

        def one_slot(r, carry):
            p = jnp.maximum(table_ref[0, r], 0)
            q = jnp.maximum(table_ref[1, r], 0)
            for g in range(groups):
                for i in range(width // lane):
                    right = [x_ref[q, i, pl.ds(g * group_rows + k, ROWS, stride=step), :] for k in range(step)]
                    real, imag = [], []
                    for a in range(stations):
                        re = im = None
                        for t in range(segs):
                            at = g * group_rows + a * step + 2 * t
                            x0 = x_ref[p, i, pl.ds(at, 1), :]
                            x1 = x_ref[p, i, pl.ds(at + 1, 1), :]
                            y0, y1 = right[2 * t], right[2 * t + 1]
                            u = x0 * y0 + x1 * y1
                            v = x1 * y0 - x0 * y1
                            re = u if re is None else re + u
                            im = v if im is None else im + v
                        real.append(re)
                        imag.append(im)
                    for a in range(0, stations, 2):
                        at = pl.multiple_of(g * rows + (r * stations + a) * ROWS, 2 * ROWS)
                        at = pl.ds(at, 2 * ROWS)
                        cross_ref[at, pl.ds(i * lane, lane)] = jnp.concatenate(real[a : a + 2], axis=0).astype(BF16)
                        cross_ref[at, pl.ds(width + i * lane, lane)] = jnp.concatenate(imag[a : a + 2], axis=0).astype(BF16)
            return carry

        lax.fori_loop(0, slots, one_slot, 0)
        lag_terms(1 - (seg_ref[0] & 1), cross_ref, k_ref, send_ref, lag_ref, groups, stations)

    return call(
        body,
        [((groups * rows, 2 * width), BF16), ((slots * stations * stations, half), F32)],
        [*blocks, kernel],
        "forward",
        [pltpu.VMEM((count, width // lane, height + spare, lane), F32), pltpu.VMEM((groups * rows, half), F32)],
        [table, sta, seg],
    )


def lag_terms(core, cross_ref, k_ref, out_ref, lag_ref, groups, stations):
    half = k_ref.shape[1] // 2
    here = pl.ds(pl.multiple_of(core * half, 128), half)
    lag_ref[...] = jnp.dot(cross_ref[...], k_ref[:, here], preferred_element_type=F32)
    rows = lag_ref.shape[0] // groups
    for k in range(rows // ROWS):
        value = lag_ref[pl.ds(k * ROWS, stations), :]
        for g in range(1, groups):
            value = value + lag_ref[pl.ds(g * rows + k * ROWS, stations), :]
        out_ref[pl.ds(k * stations, stations), :] = value


def forward_own(cross, kernel, seg, groups, stations):
    half = kernel.shape[1] // 2
    tiles = cross.shape[0] // (groups * ROWS)

    def body(seg_ref, cross_ref, k_ref, o_ref, lag_ref):
        lag_terms(seg_ref[0] & 1, cross_ref, k_ref, o_ref, lag_ref, groups, stations)

    scratch = [pltpu.VMEM((cross.shape[0], half), F32)]
    return call(body, ((tiles * stations, half), F32), [cross, kernel], "forward_own", scratch, [seg])


def misfit(a, b, observed, table, place, seg, scale):
    slots, stations, _, lags = observed.shape
    half = lags // 2

    def body(table_ref, place_ref, seg_ref, a_ref, b_ref, obs_ref, o_ref):
        here = pl.ds(pl.multiple_of((seg_ref[0] & 1) * half, 128), half)
        column = lax.broadcasted_iota(jnp.int32, (stations, half), 0)
        pad = jnp.zeros((ROWS - stations, half), F32)
        for r in range(slots):
            p, q = table_ref[0, r], table_ref[1, r]
            low = jnp.where(p < 0, stations, jnp.where(p != q, -1, 0))
            same = jnp.where(p == q, 1, 0)
            tiles = []
            for row in range(stations):
                at = pl.ds((r * stations + row) * stations, stations)
                value = jnp.tanh(scale * (a_ref[at, :] + b_ref[at, :]) - obs_ref[r, row, :, here])
                value = jnp.where(column > low + same * row, value, 0.0)
                tiles += [value, pad]
            for row in range(0, stations, 2):
                at = pl.ds((r * stations + row) * ROWS, 2 * ROWS)
                o_ref[at, :] = jnp.concatenate(tiles[2 * row : 2 * row + 4], axis=0).astype(BF16)

    return call(body, ((slots * stations * ROWS, half), BF16), [a, b, observed], "misfit", (), [table, place, seg])


def gamma_terms(residual, kernel, seg, core, name):
    rows, half = residual.shape
    depth = kernel.shape[0]
    contract = (((1,), (1,)), ((), ()))

    def body(seg_ref, r_ref, k_ref, o_ref):
        here = pl.ds(pl.multiple_of((seg_ref[0] & 1 ^ core) * half, 128), half)
        o_ref[...] = lax.dot_general(r_ref[...], k_ref[:, here], contract, preferred_element_type=F32)

    return call(body, ((rows, depth), F32), [residual, kernel], name, (), [seg])


def backward(base, other, cross, kernel, plus, minus, seg, groups, stations, scale, part):
    rows, half = other.shape
    both = kernel.shape[0] // 2
    width = both // 2
    targets = plus.shape[0]
    begin = part * width

    def body(seg_ref, base_ref, other_ref, cross_ref, k_ref, plus_ref, minus_ref, o_ref):
        there = pl.ds(pl.multiple_of((1 - (seg_ref[0] & 1)) * half, 128), half)
        residual = other_ref[...]
        contract = (((1,), (1,)), ((), ()))

        def gamma(at):
            rest = lax.dot_general(residual, k_ref[at, there], contract, preferred_element_type=F32)
            return scale * (base_ref[:, at] + rest)

        def stack(at):
            value = cross_ref[pl.ds(0, rows), at].astype(F32)
            for g in range(1, groups):
                value = value + cross_ref[pl.ds(g * rows, rows), at].astype(F32)
            return value

        def total(select, value):
            high = value.astype(BF16)
            low = (value - high.astype(F32)).astype(BF16)
            return jnp.dot(select, high, preferred_element_type=F32) + jnp.dot(
                select, low, preferred_element_type=F32
            )

        real_at, imag_at = pl.ds(begin, width), pl.ds(both + begin, width)
        real, imag = gamma(real_at), gamma(imag_at)
        stack_real, stack_imag = stack(real_at), stack(imag_at)
        common = total(plus_ref[...], real * stack_real + imag * stack_imag)
        twist = total(minus_ref[...], imag * stack_real - real * stack_imag)
        o_ref[pl.ds(0, targets), :] = common
        o_ref[pl.ds(targets, targets), :] = twist

    name = ("backward_own", "backward_mate")[part]
    operands = [base, other, cross, kernel, plus, minus]
    return call(body, ((2 * targets, width), F32), operands, name, (), [seg])


def split_low(a, b, top):
    rows, width = a.shape
    high = rows // (2 * top)

    def body(a_ref, b_ref, *refs):
        for e in range(top):
            for c in range(2):
                at = pl.ds((c * top + e) * high, high)
                refs[e][c] = a_ref[at, :] + b_ref[at, :]

    return call(body, [((2, high, width), F32)] * top, [a, b], "split_low")


def split_top(arrays):
    _, high, width = arrays[0].shape
    half = high // 2
    count = len(arrays)

    def body(*refs):
        for k in range(2):
            for c in range(2):
                at = pl.ds(k * half, half)
                value = refs[0][c, at, :]
                for ref in refs[1:count]:
                    value = value + ref[c, at, :]
                refs[count + k][c] = value

    return call(body, [((2, half, width), F32)] * 2, arrays, "split_top")


def finish(pieces):
    _, stations, width = pieces[0].shape

    def body(*refs):
        o_ref = refs[-1]
        for c in range(2):
            value = refs[0][c]
            for ref in refs[1:-1]:
                value = value + ref[c]
            for n in range(stations):
                o_ref[n, pl.ds(c, 1), :] = value[n : n + 1]

    return call(body, ((stations, 2, width), F32), pieces, "finish", inside=False)


def on_device(spectra, observed, pair_table):
    stations, segs, _, freqs = spectra.shape
    slots = pair_table.shape[0]
    lags = observed.shape[3]
    stas = lax.axis_size("sta")
    seg_devices = lax.axis_size("seg")
    groups = seg_devices // 2
    scale = 1.0 / math.sqrt(freqs * segs * seg_devices)
    seg = lax.axis_index("seg").astype(jnp.int32).reshape(1)
    sta = lax.axis_index("sta").astype(jnp.int32).reshape(1)
    table = pair_table.T

    def along_sta(x, bit):
        return swap(x, ("sta",), (stas,), (bit,))

    def along_seg(x, bit):
        return swap(x, ("seg",), (seg_devices,), (bit,))

    top = stas // 2
    parts = prepare(spectra, seg, seg_devices)
    near = [parts[0]] + [along_seg(parts[h], 2 * h) for h in range(1, groups)]
    far = [
        swap(parts[h], ("sta", "seg"), (stas, seg_devices), (top, 2 * h)) if h else along_sta(parts[h], top)
        for h in range(groups)
    ]
    moved = {0: pack(near, "pack_near"), top: pack(far, "pack_far")}
    for e in range(1, top):
        moved[e] = along_sta(moved[0], e)
    for e in range(1, top):
        moved[top + e] = along_sta(moved[top], e)
    order = [0, top, *range(1, top), *range(top + 1, stas)]
    kernel = lag_kernel(freqs, lags, seg, seg_devices)
    plus, minus, table = selection(table, sta, slots, stations, stas)

    blocks = [moved[d] for d in order]
    blocks[0], kernel, plus, minus, table = lax.optimization_barrier((blocks[0], kernel, plus, minus, table))
    cross, send = forward(blocks, order, kernel, table, sta, seg, groups, segs, stations, slots)
    sent = along_seg(send, 1)
    total = forward_own(cross, kernel, seg, groups, stations) + sent
    bit = 2
    while 2 * bit < seg_devices:
        total = total + along_seg(total, bit)
        bit *= 2
    last = along_seg(total, bit)
    residual = misfit(total, last, observed, table, sta, seg, scale)
    other = along_seg(residual, 1)
    base = gamma_terms(residual, kernel, seg, 0, "gamma_own")
    rest = (base, other, cross, kernel, plus, minus, seg, groups, stations, scale)
    send = along_seg(backward(*rest, 1), 1)
    pieces = split_low(backward(*rest, 0), send, top)
    pieces = [pieces[0]] + [along_sta(pieces[e], e) for e in (3,2,1)]
    keep, send = split_top(pieces)
    return finish([keep, along_sta(send, top)])


def solution(mesh):
    placed = (P("sta", "seg", None, None), P("sta", None, None, None), P("sta", None))
    return jax.shard_map(
        on_device, mesh=mesh, in_specs=placed, out_specs=P("sta", None, "seg"), check_vma=False
    )
```

```python
import math

import jax
import jax.numpy as jnp
from jax import lax
from jax.experimental import pallas as pl
from jax.experimental.pallas import tpu as pltpu
from jax.sharding import PartitionSpec as P

ROWS = 8
LANES = 128

F32 = jnp.float32
BF16 = jnp.bfloat16


def space(dtype):
    return pltpu.SMEM if dtype == jnp.int32 else pltpu.VMEM


def call(body, outs, operands, name, scratch=(), scalars=(), inside=True, limit=24 << 20):
    smem = pl.BlockSpec(memory_space=pltpu.SMEM)
    vmem = pl.BlockSpec(memory_space=pltpu.VMEM)
    operands = [pltpu.with_memory_space_constraint(x, pltpu.VMEM) for x in operands]
    single = isinstance(outs, tuple)
    out_list = [outs] if single else outs
    result = pl.pallas_call(
        body,
        out_shape=[space(d)(s, d) if inside else jax.ShapeDtypeStruct(s, d) for s, d in out_list],
        in_specs=[smem] * len(scalars) + [vmem] * len(operands),
        out_specs=[pl.BlockSpec(memory_space=space(d)) for _, d in out_list],
        scratch_shapes=list(scratch),
        name=name,
        compiler_params=pltpu.CompilerParams(vmem_limit_bytes=limit),
    )(*scalars, *operands)
    return result[0] if single else result


def swap(x, axes, sizes, bits):
    places = [()]
    for size in sizes:
        places = [place + (i,) for place in places for i in range(size)]

    def flat(place):
        out = 0
        for i, size in zip(place, sizes):
            out = out * size + i
        return out

    pairs = [(flat(p), flat(tuple(i ^ b for i, b in zip(p, bits)))) for p in places]
    return lax.ppermute(x, axes if len(axes) > 1 else axes[0], pairs)


def prepare(spectra, seg, seg_devices):
    stations, segs, parts, freqs = spectra.shape
    width = freqs // seg_devices
    aligned = width % 128 == 0
    if not aligned:
        chunks = spectra.reshape(stations, segs, parts, seg_devices, width)
        spectra = jnp.take(chunks, jnp.arange(seg_devices) ^ seg[0], axis=3).reshape(spectra.shape)
    rows = segs * parts * stations

    def body(seg_ref, x_ref, *refs):
        tmp = refs[-1]
        for n in range(stations):
            for t in range(segs):
                tmp[pl.ds((n * segs + t) * parts, parts), :] = x_ref[n, t].astype(F32)
        for k in range(seg_devices):
            at = pl.ds(k * width, width)
            if aligned:
                at = pl.ds(pl.multiple_of((seg_ref[0] ^ k) * width, 128), width)
            refs[k // 2][:, pl.ds(k % 2 * width, width)] = tmp[:, at].astype(BF16)

    outs = [((rows, 2 * width), BF16)] * (seg_devices // 2)
    return call(body, outs, [spectra], "prepare", [pltpu.VMEM((rows, freqs), F32)], [seg])


def pack(arrays, name):
    rows, width = arrays[0].shape

    def body(*refs):
        for k, ref in enumerate(refs[:-1]):
            refs[-1][pl.ds(k * rows, rows), :] = ref[...]

    return call(body, ((len(arrays) * rows, width), arrays[0].dtype), arrays, name)


def lag_kernel(freqs, lags, seg, seg_devices):
    width = freqs // seg_devices
    fine = math.gcd(width, 64)
    coarse = freqs // fine
    period = 2 * freqs

    def body(seg_ref, o_ref, cos_ref, sin_ref):
        def table(count, step):
            f = lax.broadcasted_iota(jnp.int32, (count, lags), 0) * step
            offset = lax.broadcasted_iota(jnp.int32, (count, lags), 1) - lags // 2
            phase = (f * offset) & (period - 1)
            angle = math.pi / freqs * phase.astype(F32)
            return jnp.cos(angle), jnp.sin(angle)

        fine_cos, fine_sin = table(fine, 1)
        big_cos, big_sin = table(coarse, fine)
        cos_ref[...] = big_cos
        sin_ref[...] = big_sin
        for k in range(2):
            for s in range(width // fine):
                row = (seg_ref[0] ^ k) * (width // fine) + s
                c = cos_ref[pl.ds(row, 1), :]
                d = sin_ref[pl.ds(row, 1), :]
                at = k * width + s * fine
                o_ref[pl.ds(at, fine), :] = (fine_cos * c - fine_sin * d).astype(BF16)
                o_ref[pl.ds(2 * width + at, fine), :] = (-(fine_sin * c + fine_cos * d)).astype(BF16)

    scratch = [pltpu.VMEM((coarse, lags), F32)] * 2
    return call(body, ((4 * width, lags), BF16), [], "lag_kernel", scratch, [seg])


def selection(table, sta, slots, stations, blocks):
    rows = slots * stations * ROWS
    targets = blocks * stations
    top = blocks // 2

    def body(table_ref, sta_ref, plus_ref, minus_ref, keep_ref):
        for i in range(2):
            for s in range(slots):
                keep_ref[i, s] = table_ref[i, s]
        m = lax.broadcasted_iota(jnp.int32, (targets, rows), 0)
        n = m % stations
        group = m // stations
        block = sta_ref[0] ^ (top * (group % 2) + group // 2)
        k = lax.broadcasted_iota(jnp.int32, (targets, rows), 1)
        b = k % ROWS
        a = (k // ROWS) % stations
        r = k // (ROWS * stations)
        first = jnp.full((targets, rows), -1, jnp.int32)
        second = jnp.full((targets, rows), -1, jnp.int32)
        for s in range(slots):
            first = jnp.where(r == s, table_ref[0, s], first)
            second = jnp.where(r == s, table_ref[1, s], second)
        left = jnp.where((first == block) & (a == n), 1.0, 0.0)
        right = jnp.where((second == block) & (b == n), 1.0, 0.0)
        plus_ref[...] = (left + right).astype(BF16)
        minus_ref[...] = (left - right).astype(BF16)

    outs = [((targets, rows), BF16), ((targets, rows), BF16), (table.shape, jnp.int32)]
    return call(body, outs, [], "selection", (), [table, sta])


def unpack(blocks, order, sta, stations, segs):
    count = len(blocks)
    height, width = blocks[0].shape
    spare = (ROWS - stations) * 2 * segs

    def body(sta_ref, *refs):
        for k, d in enumerate(order):
            at = sta_ref[0] ^ d
            for i in range(width // LANES):
                refs[-1][at, i, pl.ds(0, height), :] = refs[k][:, pl.ds(i * LANES, LANES)].astype(F32)
                refs[-1][at, i, pl.ds(height, spare), :] = jnp.zeros((spare, LANES), F32)

    return call(body, ((count, width // LANES, height + spare, LANES), F32), blocks, "unpack", (), [sta])


def forward(spectra, kernel, table, seg, groups, segs, stations, begin, end):
    tiles = spectra.shape[1]
    width = tiles * LANES
    step = 2 * segs
    group_rows = stations * step
    half = kernel.shape[1] // 2
    slots = end - begin
    rows = slots * stations * ROWS

    def body(table_ref, seg_ref, x_ref, k_ref, cross_ref, send_ref, lag_ref):
        def one_slot(r, carry):
            p = jnp.maximum(table_ref[0, begin + r], 0)
            q = jnp.maximum(table_ref[1, begin + r], 0)
            for g in range(groups):
                for i in range(tiles):
                    right = [x_ref[q, i, pl.ds(g * group_rows + k, ROWS, stride=step), :] for k in range(step)]
                    real, imag = [], []
                    for a in range(stations):
                        re = im = None
                        for t in range(segs):
                            at = g * group_rows + a * step + 2 * t
                            x0 = x_ref[p, i, pl.ds(at, 1), :]
                            x1 = x_ref[p, i, pl.ds(at + 1, 1), :]
                            y0, y1 = right[2 * t], right[2 * t + 1]
                            u = x0 * y0 + x1 * y1
                            v = x1 * y0 - x0 * y1
                            re = u if re is None else re + u
                            im = v if im is None else im + v
                        real.append(re)
                        imag.append(im)
                    for a in range(0, stations, 2):
                        at = pl.multiple_of(g * rows + (r * stations + a) * ROWS, 2 * ROWS)
                        at = pl.ds(at, 2 * ROWS)
                        cross_ref[at, pl.ds(i * LANES, LANES)] = jnp.concatenate(real[a : a + 2], axis=0).astype(BF16)
                        cross_ref[at, pl.ds(width + i * LANES, LANES)] = jnp.concatenate(
                            imag[a : a + 2], axis=0
                        ).astype(BF16)
            return carry

        lax.fori_loop(0, slots, one_slot, 0)
        lag_terms(1 - (seg_ref[0] & 1), cross_ref, k_ref, send_ref, lag_ref, groups, stations)

    return call(
        body,
        [((groups * rows, 2 * width), BF16), ((slots * stations * stations, half), F32)],
        [spectra, kernel],
        "forward_mate",
        [pltpu.VMEM((groups * rows, half), F32)],
        [table, seg],
    )


def lag_terms(core, cross_ref, k_ref, out_ref, lag_ref, groups, stations):
    half = k_ref.shape[1] // 2
    here = pl.ds(pl.multiple_of(core * half, 128), half)
    lag_ref[...] = jnp.dot(cross_ref[...], k_ref[:, here], preferred_element_type=F32)
    rows = lag_ref.shape[0] // groups
    for k in range(rows // ROWS):
        value = lag_ref[pl.ds(k * ROWS, stations), :]
        for g in range(1, groups):
            value = value + lag_ref[pl.ds(g * rows + k * ROWS, stations), :]
        out_ref[pl.ds(k * stations, stations), :] = value


def forward_own(cross, kernel, seg, groups, stations):
    half = kernel.shape[1] // 2
    tiles = cross.shape[0] // (groups * ROWS)

    def body(seg_ref, cross_ref, k_ref, o_ref, lag_ref):
        lag_terms(seg_ref[0] & 1, cross_ref, k_ref, o_ref, lag_ref, groups, stations)

    scratch = [pltpu.VMEM((cross.shape[0], half), F32)]
    return call(body, ((tiles * stations, half), F32), [cross, kernel], "forward_own", scratch, [seg])


def misfit(a, b, observed, table, seg, scale, begin, end):
    _, stations, _, lags = observed.shape
    half = lags // 2
    slots = end - begin

    def body(table_ref, seg_ref, a_ref, b_ref, obs_ref, o_ref):
        here = pl.ds(pl.multiple_of((seg_ref[0] & 1) * half, 128), half)
        column = lax.broadcasted_iota(jnp.int32, (stations, half), 0)
        pad = jnp.zeros((ROWS - stations, half), F32)
        for r in range(slots):
            p, q = table_ref[0, begin + r], table_ref[1, begin + r]
            low = jnp.where(p < 0, stations, jnp.where(p != q, -1, 0))
            same = jnp.where(p == q, 1, 0)
            tiles = []
            for row in range(stations):
                at = pl.ds((r * stations + row) * stations, stations)
                value = jnp.tanh(scale * (a_ref[at, :] + b_ref[at, :]) - obs_ref[begin + r, row, :, here])
                value = jnp.where(column > low + same * row, value, 0.0)
                tiles += [value, pad]
            for row in range(0, stations, 2):
                at = pl.ds((r * stations + row) * ROWS, 2 * ROWS)
                o_ref[at, :] = jnp.concatenate(tiles[2 * row : 2 * row + 4], axis=0).astype(BF16)

    return call(body, ((slots * stations * ROWS, half), BF16), [a, b, observed], "misfit", (), [table, seg])


def gamma_own(residual, kernel, seg):
    rows, half = residual.shape
    width = kernel.shape[0] // 4
    contract = (((1,), (1,)), ((), ()))

    def body(seg_ref, r_ref, k_ref, o_ref):
        here = pl.ds(pl.multiple_of((seg_ref[0] & 1) * half, 128), half)
        for c in range(2):
            part = k_ref[pl.ds(2 * c * width, width), here]
            o_ref[c] = lax.dot_general(r_ref[...], part, contract, preferred_element_type=F32)

    return call(body, ((2, rows, width), F32), [residual, kernel], "gamma_own", (), [seg])


def pick_mate(crosses):
    part = crosses[0].shape[1] // 4
    rows = sum(cross.shape[0] for cross in crosses)

    def body(*refs):
        top = 0
        for ref in refs[:-1]:
            at = pl.ds(top, ref.shape[0])
            for c in range(2):
                refs[-1][c, at, :] = ref[:, pl.ds((2 * c + 1) * part, part)]
            top += ref.shape[0]

    return call(body, ((2, rows, part), BF16), crosses, "pick_mate")


def backward(pieces, mates, kernel, plus, minus, seg, groups, scale):
    width = kernel.shape[0] // 4
    half = kernel.shape[1] // 2
    targets, total_rows = plus.shape
    heights = [piece[1].shape[0] for piece in pieces]
    count = 3 * len(pieces)

    def body(seg_ref, *refs):
        mate_ref, k_ref, plus_ref, minus_ref, o_ref, common_ref, twist_ref = refs[count:]
        there = pl.ds(pl.multiple_of((1 - (seg_ref[0] & 1)) * half, 128), half)
        contract = (((1,), (1,)), ((), ()))
        top = 0
        for i, rows in enumerate(heights):
            base_ref, other_ref, cross_ref = refs[3 * i : 3 * i + 3]
            residual = other_ref[...]
            gamma, stack = [], []
            for c in range(2):
                part = k_ref[pl.ds(2 * c * width, width), there]
                rest = lax.dot_general(residual, part, contract, preferred_element_type=F32)
                gamma.append(scale * (base_ref[c] + rest))
                value = None
                for g in range(groups):
                    pair = cross_ref[pl.ds(g * rows, rows), pl.ds(2 * c * width, width)].astype(F32)
                    pair = pair + mate_ref[c, pl.ds(groups * top + g * rows, rows), :].astype(F32)
                    value = pair if value is None else value + pair
                stack.append(value)
            common = gamma[0] * stack[0] + gamma[1] * stack[1]
            twist = gamma[1] * stack[0] - gamma[0] * stack[1]
            for ref, value in ((common_ref, common), (twist_ref, twist)):
                high = value.astype(BF16)
                ref[0, pl.ds(top, rows), :] = high
                ref[1, pl.ds(top, rows), :] = (value - high.astype(F32)).astype(BF16)
            top += rows
        for c, (select, ref) in enumerate(((plus_ref[...], common_ref), (minus_ref[...], twist_ref))):
            high = jnp.dot(select, ref[0], preferred_element_type=F32)
            o_ref[pl.ds(c * targets, targets), :] = high + jnp.dot(select, ref[1], preferred_element_type=F32)

    operands = [x for piece in pieces for x in piece] + [mates, kernel, plus, minus]
    scratch = [pltpu.VMEM((2, total_rows, width), BF16)] * 2
    return call(body, ((2 * targets, width), F32), operands, "backward", scratch, [seg])


def split_low(a, top):
    rows, width = a.shape
    high = rows // (2 * top)

    def body(a_ref, *refs):
        for e in range(top):
            for c in range(2):
                at = pl.ds((c * top + e) * high, high)
                refs[e][c] = a_ref[at, :]

    return call(body, [((2, high, width), F32)] * top, [a], "split_low")


def split_top(arrays):
    _, high, width = arrays[0].shape
    half = high // 2
    count = len(arrays)

    def body(*refs):
        for k in range(2):
            for c in range(2):
                at = pl.ds(k * half, half)
                value = refs[0][c, at, :]
                for ref in refs[1:count]:
                    value = value + ref[c, at, :]
                refs[count + k][c] = value

    return call(body, [((2, half, width), F32)] * 2, arrays, "split_top")


def finish(pieces):
    _, stations, width = pieces[0].shape

    def body(*refs):
        o_ref = refs[-1]
        for c in range(2):
            value = refs[0][c]
            for ref in refs[1:-1]:
                value = value + ref[c]
            for n in range(stations):
                o_ref[n, pl.ds(c, 1), :] = value[n : n + 1]

    return call(body, ((stations, 2, width), F32), pieces, "finish", inside=False)


def on_device(spectra, observed, pair_table):
    stations, segs, _, freqs = spectra.shape
    slots = pair_table.shape[0]
    lags = observed.shape[3]
    stas = lax.axis_size("sta")
    seg_devices = lax.axis_size("seg")
    groups = seg_devices // 2
    scale = 1.0 / math.sqrt(freqs * segs * seg_devices)
    seg = lax.axis_index("seg").astype(jnp.int32).reshape(1)
    sta = lax.axis_index("sta").astype(jnp.int32).reshape(1)
    table = pair_table.T

    def along_sta(x, bit):
        return swap(x, ("sta",), (stas,), (bit,))

    def along_seg(x, bit):
        return swap(x, ("seg",), (seg_devices,), (bit,))

    top = stas // 2
    parts = prepare(spectra, seg, seg_devices)
    near = [parts[0]] + [along_seg(parts[h], 2 * h) for h in range(1, groups)]
    far = [
        swap(parts[h], ("sta", "seg"), (stas, seg_devices), (top, 2 * h)) if h else along_sta(parts[h], top)
        for h in range(groups)
    ]
    moved = {0: pack(near, "pack_near"), top: pack(far, "pack_far")}
    for e in range(1, top):
        moved[e] = along_sta(moved[0], e)
    for e in range(1, top):
        moved[top + e] = along_sta(moved[top], e)
    order = [0, top, *range(1, top), *range(top + 1, stas)]
    kernel = lag_kernel(freqs, lags, seg, seg_devices)
    plus, minus, table = selection(table, sta, slots, stations, stas)

    blocks = [moved[d] for d in order]
    blocks[0], kernel, plus, minus, table = lax.optimization_barrier((blocks[0], kernel, plus, minus, table))
    spectra = unpack(blocks, order, sta, stations, segs)
    cut = slots // 2
    parts = []
    for begin, end in ((0, cut), (cut, slots)):
        cross, send = forward(spectra, kernel, table, seg, groups, segs, stations, begin, end)
        sent = along_seg(send, 1)
        total = forward_own(cross, kernel, seg, groups, stations) + sent
        bit = 2
        while 2 * bit < seg_devices:
            total = total + along_seg(total, bit)
            bit *= 2
        parts.append((begin, end, cross, total, along_seg(total, bit)))
    crosses, _ = lax.optimization_barrier(([part[2] for part in parts], parts[-1][3]))
    mates = along_seg(pick_mate(crosses), 1)
    pieces = []
    for begin, end, cross, total, last in parts:
        residual = misfit(total, last, observed, table, seg, scale, begin, end)
        other = along_seg(residual, 1)
        pieces.append((gamma_own(residual, kernel, seg), other, cross))
    pieces = split_low(backward(pieces, mates, kernel, plus, minus, seg, groups, scale), top)
    pieces = [pieces[0]] + [along_sta(pieces[e], e) for e in (3,2,1)]
    keep, send = split_top(pieces)
    return finish([keep, along_sta(send, top)])


def solution(mesh):
    placed = (P("sta", "seg", None, None), P("sta", None, None, None), P("sta", None))
    return jax.shard_map(
        on_device, mesh=mesh, in_specs=placed, out_specs=P("sta", None, "seg"), check_vma=False
    )
```

```python
import math

import jax
import jax.numpy as jnp
from jax import lax
from jax.experimental import pallas as pl
from jax.experimental.pallas import tpu as pltpu
from jax.sharding import PartitionSpec as P

ROWS = 8
LANES = 128

F32 = jnp.float32
BF16 = jnp.bfloat16


def space(dtype):
    return pltpu.SMEM if dtype == jnp.int32 else pltpu.VMEM


def call(body, outs, operands, name, scratch=(), scalars=(), inside=True, limit=24 << 20):
    smem = pl.BlockSpec(memory_space=pltpu.SMEM)
    vmem = pl.BlockSpec(memory_space=pltpu.VMEM)
    operands = [pltpu.with_memory_space_constraint(x, pltpu.VMEM) for x in operands]
    single = isinstance(outs, tuple)
    out_list = [outs] if single else outs
    result = pl.pallas_call(
        body,
        out_shape=[space(d)(s, d) if inside else jax.ShapeDtypeStruct(s, d) for s, d in out_list],
        in_specs=[smem] * len(scalars) + [vmem] * len(operands),
        out_specs=[pl.BlockSpec(memory_space=space(d)) for _, d in out_list],
        scratch_shapes=list(scratch),
        name=name,
        compiler_params=pltpu.CompilerParams(vmem_limit_bytes=limit),
    )(*scalars, *operands)
    return result[0] if single else result


def swap(x, axes, sizes, bits):
    places = [()]
    for size in sizes:
        places = [place + (i,) for place in places for i in range(size)]

    def flat(place):
        out = 0
        for i, size in zip(place, sizes):
            out = out * size + i
        return out

    pairs = [(flat(p), flat(tuple(i ^ b for i, b in zip(p, bits)))) for p in places]
    return lax.ppermute(x, axes if len(axes) > 1 else axes[0], pairs)


def prepare(spectra, seg, seg_devices):
    stations, segs, parts, freqs = spectra.shape
    width = freqs // seg_devices
    aligned = width % 128 == 0
    if not aligned:
        chunks = spectra.reshape(stations, segs, parts, seg_devices, width)
        spectra = jnp.take(chunks, jnp.arange(seg_devices) ^ seg[0], axis=3).reshape(spectra.shape)
    rows = segs * parts * stations

    def body(seg_ref, x_ref, *refs):
        tmp = refs[-1]
        for n in range(stations):
            for t in range(segs):
                tmp[pl.ds((n * segs + t) * parts, parts), :] = x_ref[n, t].astype(F32)
        for k in range(seg_devices):
            at = pl.ds(k * width, width)
            if aligned:
                at = pl.ds(pl.multiple_of((seg_ref[0] ^ k) * width, 128), width)
            refs[k // 2][:, pl.ds(k % 2 * width, width)] = tmp[:, at].astype(BF16)

    outs = [((rows, 2 * width), BF16)] * (seg_devices // 2)
    return call(body, outs, [spectra], "prepare", [pltpu.VMEM((rows, freqs), F32)], [seg])


def pack(arrays, name):
    rows, width = arrays[0].shape

    def body(*refs):
        for k, ref in enumerate(refs[:-1]):
            refs[-1][pl.ds(k * rows, rows), :] = ref[...]

    return call(body, ((len(arrays) * rows, width), arrays[0].dtype), arrays, name)


def lag_kernel(freqs, lags, seg, seg_devices):
    width = freqs // seg_devices
    fine = math.gcd(width, 64)
    coarse = freqs // fine
    period = 2 * freqs

    def body(seg_ref, o_ref, cos_ref, sin_ref):
        def table(count, step):
            f = lax.broadcasted_iota(jnp.int32, (count, lags), 0) * step
            offset = lax.broadcasted_iota(jnp.int32, (count, lags), 1) - lags // 2
            phase = (f * offset) & (period - 1)
            angle = math.pi / freqs * phase.astype(F32)
            return jnp.cos(angle), jnp.sin(angle)

        fine_cos, fine_sin = table(fine, 1)
        big_cos, big_sin = table(coarse, fine)
        cos_ref[...] = big_cos
        sin_ref[...] = big_sin
        for k in range(2):
            for s in range(width // fine):
                row = (seg_ref[0] ^ k) * (width // fine) + s
                c = cos_ref[pl.ds(row, 1), :]
                d = sin_ref[pl.ds(row, 1), :]
                at = k * width + s * fine
                o_ref[pl.ds(at, fine), :] = (fine_cos * c - fine_sin * d).astype(BF16)
                o_ref[pl.ds(2 * width + at, fine), :] = (-(fine_sin * c + fine_cos * d)).astype(BF16)

    scratch = [pltpu.VMEM((coarse, lags), F32)] * 2
    return call(body, ((4 * width, lags), BF16), [], "lag_kernel", scratch, [seg])


def selection(table, sta, slots, stations, blocks):
    rows = slots * stations * ROWS
    targets = blocks * stations
    top = blocks // 2

    def body(table_ref, sta_ref, plus_ref, minus_ref, keep_ref):
        for i in range(2):
            for s in range(slots):
                keep_ref[i, s] = table_ref[i, s]
        m = lax.broadcasted_iota(jnp.int32, (targets, rows), 0)
        n = m % stations
        group = m // stations
        block = sta_ref[0] ^ (top * (group % 2) + group // 2)
        k = lax.broadcasted_iota(jnp.int32, (targets, rows), 1)
        b = k % ROWS
        a = (k // ROWS) % stations
        r = k // (ROWS * stations)
        first = jnp.full((targets, rows), -1, jnp.int32)
        second = jnp.full((targets, rows), -1, jnp.int32)
        for s in range(slots):
            first = jnp.where(r == s, table_ref[0, s], first)
            second = jnp.where(r == s, table_ref[1, s], second)
        left = jnp.where((first == block) & (a == n), 1.0, 0.0)
        right = jnp.where((second == block) & (b == n), 1.0, 0.0)
        plus_ref[...] = (left + right).astype(BF16)
        minus_ref[...] = (left - right).astype(BF16)

    outs = [((targets, rows), BF16), ((targets, rows), BF16), (table.shape, jnp.int32)]
    return call(body, outs, [], "selection", (), [table, sta])


def unpack(blocks, order, sta, stations, segs):
    count = len(blocks)
    height, width = blocks[0].shape
    spare = (ROWS - stations) * 2 * segs

    def body(sta_ref, *refs):
        for k, d in enumerate(order):
            at = sta_ref[0] ^ d
            for i in range(width // LANES):
                refs[-1][at, i, pl.ds(0, height), :] = refs[k][:, pl.ds(i * LANES, LANES)].astype(F32)
                refs[-1][at, i, pl.ds(height, spare), :] = jnp.zeros((spare, LANES), F32)

    return call(body, ((count, width // LANES, height + spare, LANES), F32), blocks, "unpack", (), [sta])


def forward(spectra, kernel, table, seg, groups, segs, stations, begin, end):
    tiles = spectra.shape[1]
    width = tiles * LANES
    step = 2 * segs
    group_rows = stations * step
    half = kernel.shape[1] // 2
    slots = end - begin
    rows = slots * stations * ROWS

    def body(table_ref, seg_ref, x_ref, k_ref, cross_ref, send_ref, lag_ref):
        def one_slot(r, carry):
            p = jnp.maximum(table_ref[0, begin + r], 0)
            q = jnp.maximum(table_ref[1, begin + r], 0)
            for g in range(groups):
                for i in range(tiles):
                    right = [x_ref[q, i, pl.ds(g * group_rows + k, ROWS, stride=step), :] for k in range(step)]
                    real, imag = [], []
                    for a in range(stations):
                        re = im = None
                        for t in range(segs):
                            at = g * group_rows + a * step + 2 * t
                            x0 = x_ref[p, i, pl.ds(at, 1), :]
                            x1 = x_ref[p, i, pl.ds(at + 1, 1), :]
                            y0, y1 = right[2 * t], right[2 * t + 1]
                            u = x0 * y0 + x1 * y1
                            v = x1 * y0 - x0 * y1
                            re = u if re is None else re + u
                            im = v if im is None else im + v
                        real.append(re)
                        imag.append(im)
                    for a in range(0, stations, 2):
                        at = pl.multiple_of(g * rows + (r * stations + a) * ROWS, 2 * ROWS)
                        at = pl.ds(at, 2 * ROWS)
                        cross_ref[at, pl.ds(i * LANES, LANES)] = jnp.concatenate(real[a : a + 2], axis=0).astype(BF16)
                        cross_ref[at, pl.ds(width + i * LANES, LANES)] = jnp.concatenate(
                            imag[a : a + 2], axis=0
                        ).astype(BF16)
            return carry

        lax.fori_loop(0, slots, one_slot, 0)
        lag_terms(1 - (seg_ref[0] & 1), cross_ref, k_ref, send_ref, lag_ref, groups, stations)

    return call(
        body,
        [((groups * rows, 2 * width), BF16), ((slots * stations * stations, half), F32)],
        [spectra, kernel],
        "forward_mate",
        [pltpu.VMEM((groups * rows, half), F32)],
        [table, seg],
    )


def lag_terms(core, cross_ref, k_ref, out_ref, lag_ref, groups, stations):
    half = k_ref.shape[1] // 2
    here = pl.ds(pl.multiple_of(core * half, 128), half)
    lag_ref[...] = jnp.dot(cross_ref[...], k_ref[:, here], preferred_element_type=F32)
    rows = lag_ref.shape[0] // groups
    for k in range(rows // ROWS):
        value = lag_ref[pl.ds(k * ROWS, stations), :]
        for g in range(1, groups):
            value = value + lag_ref[pl.ds(g * rows + k * ROWS, stations), :]
        out_ref[pl.ds(k * stations, stations), :] = value


def forward_own(cross, kernel, seg, groups, stations):
    half = kernel.shape[1] // 2
    tiles = cross.shape[0] // (groups * ROWS)

    def body(seg_ref, cross_ref, k_ref, o_ref, lag_ref):
        lag_terms(seg_ref[0] & 1, cross_ref, k_ref, o_ref, lag_ref, groups, stations)

    scratch = [pltpu.VMEM((cross.shape[0], half), F32)]
    return call(body, ((tiles * stations, half), F32), [cross, kernel], "forward_own", scratch, [seg])


def misfit(a, b, observed, table, seg, scale, begin, end):
    _, stations, _, lags = observed.shape
    half = lags // 2
    slots = end - begin

    def body(table_ref, seg_ref, a_ref, b_ref, obs_ref, o_ref):
        here = pl.ds(pl.multiple_of((seg_ref[0] & 1) * half, 128), half)
        column = lax.broadcasted_iota(jnp.int32, (stations, half), 0)
        pad = jnp.zeros((ROWS - stations, half), F32)
        for r in range(slots):
            p, q = table_ref[0, begin + r], table_ref[1, begin + r]
            low = jnp.where(p < 0, stations, jnp.where(p != q, -1, 0))
            same = jnp.where(p == q, 1, 0)
            tiles = []
            for row in range(stations):
                at = pl.ds((r * stations + row) * stations, stations)
                value = jnp.tanh(scale * (a_ref[at, :] + b_ref[at, :]) - obs_ref[begin + r, row, :, here])
                value = jnp.where(column > low + same * row, value, 0.0)
                tiles += [value, pad]
            for row in range(0, stations, 2):
                at = pl.ds((r * stations + row) * ROWS, 2 * ROWS)
                o_ref[at, :] = jnp.concatenate(tiles[2 * row : 2 * row + 4], axis=0).astype(BF16)

    return call(body, ((slots * stations * ROWS, half), BF16), [a, b, observed], "misfit", (), [table, seg])


def gamma_own(residual, kernel, seg):
    rows, half = residual.shape
    width = kernel.shape[0] // 4
    contract = (((1,), (1,)), ((), ()))

    def body(seg_ref, r_ref, k_ref, o_ref):
        here = pl.ds(pl.multiple_of((seg_ref[0] & 1) * half, 128), half)
        for c in range(2):
            part = k_ref[pl.ds(2 * c * width, width), here]
            o_ref[c] = lax.dot_general(r_ref[...], part, contract, preferred_element_type=F32)

    return call(body, ((2, rows, width), F32), [residual, kernel], "gamma_own", (), [seg])


def pick_mate(crosses):
    part = crosses[0].shape[1] // 4
    rows = sum(cross.shape[0] for cross in crosses)

    def body(*refs):
        top = 0
        for ref in refs[:-1]:
            at = pl.ds(top, ref.shape[0])
            for c in range(2):
                refs[-1][c, at, :] = ref[:, pl.ds((2 * c + 1) * part, part)]
            top += ref.shape[0]

    return call(body, ((2, rows, part), BF16), crosses, "pick_mate")


def backward(pieces, mates, kernel, plus, minus, seg, groups, scale):
    width = kernel.shape[0] // 4
    half = kernel.shape[1] // 2
    targets, total_rows = plus.shape
    heights = [piece[1].shape[0] for piece in pieces]
    count = 3 * len(pieces)

    def body(seg_ref, *refs):
        mate_ref, k_ref, plus_ref, minus_ref, o_ref, common_ref, twist_ref = refs[count:]
        there = pl.ds(pl.multiple_of((1 - (seg_ref[0] & 1)) * half, 128), half)
        contract = (((1,), (1,)), ((), ()))
        top = 0
        for i, rows in enumerate(heights):
            base_ref, other_ref, cross_ref = refs[3 * i : 3 * i + 3]
            residual = other_ref[...]
            gamma, stack = [], []
            for c in range(2):
                part = k_ref[pl.ds(2 * c * width, width), there]
                rest = lax.dot_general(residual, part, contract, preferred_element_type=F32)
                gamma.append(scale * (base_ref[c] + rest))
                value = None
                for g in range(groups):
                    pair = cross_ref[pl.ds(g * rows, rows), pl.ds(2 * c * width, width)].astype(F32)
                    pair = pair + mate_ref[c, pl.ds(groups * top + g * rows, rows), :].astype(F32)
                    value = pair if value is None else value + pair
                stack.append(value)
            common = gamma[0] * stack[0] + gamma[1] * stack[1]
            twist = gamma[1] * stack[0] - gamma[0] * stack[1]
            for ref, value in ((common_ref, common), (twist_ref, twist)):
                high = value.astype(BF16)
                ref[0, pl.ds(top, rows), :] = high
                ref[1, pl.ds(top, rows), :] = (value - high.astype(F32)).astype(BF16)
            top += rows
        for c, (select, ref) in enumerate(((plus_ref[...], common_ref), (minus_ref[...], twist_ref))):
            high = jnp.dot(select, ref[0], preferred_element_type=F32)
            o_ref[pl.ds(c * targets, targets), :] = high + jnp.dot(select, ref[1], preferred_element_type=F32)

    operands = [x for piece in pieces for x in piece] + [mates, kernel, plus, minus]
    scratch = [pltpu.VMEM((2, total_rows, width), BF16)] * 2
    return call(body, ((2 * targets, width), F32), operands, "backward", scratch, [seg])


def split_low(a, top):
    rows, width = a.shape
    high = rows // (2 * top)

    def body(a_ref, *refs):
        for e in range(top):
            for c in range(2):
                at = pl.ds((c * top + e) * high, high)
                refs[e][c] = a_ref[at, :]

    return call(body, [((2, high, width), F32)] * top, [a], "split_low")


def split_top(arrays):
    _, high, width = arrays[0].shape
    half = high // 2
    count = len(arrays)

    def body(*refs):
        for k in range(2):
            for c in range(2):
                at = pl.ds(k * half, half)
                value = refs[0][c, at, :]
                for ref in refs[1:count]:
                    value = value + ref[c, at, :]
                refs[count + k][c] = value

    return call(body, [((2, half, width), F32)] * 2, arrays, "split_top")


def finish(pieces):
    _, stations, width = pieces[0].shape

    def body(*refs):
        o_ref = refs[-1]
        for c in range(2):
            value = refs[0][c]
            for ref in refs[1:-1]:
                value = value + ref[c]
            for n in range(stations):
                o_ref[n, pl.ds(c, 1), :] = value[n : n + 1]

    return call(body, ((stations, 2, width), F32), pieces, "finish", inside=False)


def on_device(spectra, observed, pair_table):
    stations, segs, _, freqs = spectra.shape
    slots = pair_table.shape[0]
    lags = observed.shape[3]
    stas = lax.axis_size("sta")
    seg_devices = lax.axis_size("seg")
    groups = seg_devices // 2
    scale = 1.0 / math.sqrt(freqs * segs * seg_devices)
    seg = lax.axis_index("seg").astype(jnp.int32).reshape(1)
    sta = lax.axis_index("sta").astype(jnp.int32).reshape(1)
    table = pair_table.T

    def along_sta(x, bit):
        return swap(x, ("sta",), (stas,), (bit,))

    def along_seg(x, bit):
        return swap(x, ("seg",), (seg_devices,), (bit,))

    top = stas // 2
    parts = prepare(spectra, seg, seg_devices)
    near = [parts[0]] + [along_seg(parts[h], 2 * h) for h in range(1, groups)]
    far = [
        swap(parts[h], ("sta", "seg"), (stas, seg_devices), (top, 2 * h)) if h else along_sta(parts[h], top)
        for h in range(groups)
    ]
    moved = {0: pack(near, "pack_near"), top: pack(far, "pack_far")}
    for e in range(1, top):
        moved[e] = along_sta(moved[0], e)
    for e in range(1, top):
        moved[top + e] = along_sta(moved[top], e)
    order = [0, top, *range(1, top), *range(top + 1, stas)]
    kernel = lag_kernel(freqs, lags, seg, seg_devices)
    plus, minus, table = selection(table, sta, slots, stations, stas)

    blocks = [moved[d] for d in order]
    blocks[0], kernel, plus, minus, table = lax.optimization_barrier((blocks[0], kernel, plus, minus, table))
    spectra = unpack(blocks, order, sta, stations, segs)
    cut = slots // 2
    parts = []
    for begin, end in ((0, cut), (cut, slots)):
        cross, send = forward(spectra, kernel, table, seg, groups, segs, stations, begin, end)
        sent = along_seg(send, 1)
        total = forward_own(cross, kernel, seg, groups, stations) + sent
        bit = 2
        while 2 * bit < seg_devices:
            total = total + along_seg(total, bit)
            bit *= 2
        parts.append((begin, end, cross, total, along_seg(total, bit)))
    crosses, _ = lax.optimization_barrier(([part[2] for part in parts], parts[-1][3]))
    mates = along_seg(pick_mate(crosses), 1)
    pieces = []
    for begin, end, cross, total, last in parts:
        residual = misfit(total, last, observed, table, seg, scale, begin, end)
        other = along_seg(residual, 1)
        pieces.append((gamma_own(residual, kernel, seg), other, cross))
    pieces = split_low(backward(pieces, mates, kernel, plus, minus, seg, groups, scale), top)
    pieces = [pieces[0]] + [along_sta(pieces[e], e) for e in range(top - 1, 0, -1)]
    keep, send = split_top(pieces)
    return finish([keep, along_sta(send, top)])


def solution(mesh):
    placed = (P("sta", "seg", None, None), P("sta", None, None, None), P("sta", None))
    return jax.shard_map(
        on_device, mesh=mesh, in_specs=placed, out_specs=P("sta", None, "seg"), check_vma=False
    )
```
